512 devices in a mesh: view: 8 (over y_lo, core), tm: 64 (over y_hi, z, x).
Axes of the slice: x: 4, y: 8 (y_hi: 2, y_lo: 4; y = y_hi * 4 + y_lo), z: 8, core: 2. Of those that a mesh axis runs over, the one named last changes fastest.
Arguments:
- frames_x: bfloat16 [8, 64, 384, 1152], P('view', 'tm'), may hold values from -6 to 6
- box_embed: bfloat16 [8, 64, 16, 1152], P('view', 'tm'), may hold values from -6 to 6
- box_count: int32 [8, 64], P('view', 'tm'), may hold values from 1 to 16
- frame_valid: int32 [8, 64], P('view', 'tm'), may hold values 0 or 1
- cycle_link: int32 [8, 2], P('view'), may hold values 0 or 1
- w_qkv: bfloat16 [1152, 3456], P('tm'), may hold values from -0.47140452 to 0.47140452
- w_out: bfloat16 [1152, 1152], P('tm'), may hold values from -0.1875 to 0.1875
- box_gate: float32 [288], replicated, may hold values from -2 to 2
Outputs:
- mixed: bfloat16 [8, 64, 384, 1152], P('view', 'tm')
The draws below stay inside these ranges and needn't reach their ends.
All inputs are finite; a program needn't handle non-finite values. No bound on the sum of `frame_valid` or of `cycle_link` on one device may be relied on, other than what follows from the above.
Results may differ from the reference program's by a relative error of at most 0.0045.
The reference program's roundings to bfloat16 on the way (of `qkv`, `box_kv` and `attn`) count: a program that leaves them out, or rounds other values in their place, can miss the bound.
Values may be sent and summed in bfloat16 or wider, within the bound.
A program may use at most 128 MiB of HBM per device.

```python
import jax
import jax.numpy as jnp
from jax import lax

D = 1152
HD = 72
CROSS_HEADS = 8
TIME_HEADS = 4
BOX_HEADS = 4
P_SIZE = 384
NB = 16
NV = 8
FRAMES = 64


def draw_frames_x(key, part):

    def camera_draw(camera):
        camera_key = jax.random.fold_in(jax.random.fold_in(key, 101), camera)
        noise = jax.random.normal(jax.random.fold_in(camera_key, 1), (FRAMES, P_SIZE, D), jnp.float32)
        noise = jnp.clip(noise, -6.0, 6.0)
        return noise.astype(jnp.bfloat16)
    return lax.map(camera_draw, jnp.arange(NV, dtype=jnp.int32))


def draw_w_qkv(key, part):
    base = jax.random.normal(jax.random.fold_in(key, 3), (D, 3 * D), jnp.float32)
    base = jnp.clip(base, -6.0, 6.0) * D ** (-0.5)
    return base.astype(jnp.bfloat16)


def with_ends(values, key, least, high):
    longest = values.shape.index(max(values.shape))
    spots = []
    for shift in (0, 1):
        where = [jax.random.randint(jax.random.fold_in(key, axis), (), 0, length) for axis, length in enumerate(values.shape)]
        where[longest] = (where[longest] + shift) % values.shape[longest]
        spots.append(tuple(where))
    return values.at[spots[0]].set(least).at[spots[1]].set(high)


def levels(key, dims, cuts, smallest, high):
    def one(axis_at, parts):
        heights = jax.random.uniform(jax.random.fold_in(jax.random.fold_in(key, 6), axis_at), (parts,), jnp.float32, smallest / len(cuts), high / len(cuts))
        return jnp.repeat(jnp.exp(heights), dims[axis_at] // parts).reshape((-1,) + (1,) * (len(dims) - axis_at - 1))

    loudness = one(*cuts[0])
    for cut in cuts[1:]:
        loudness = loudness * one(*cut)
    return loudness


def scatter_about(rng, extent, spread, limit, cuts=(), held_as=jnp.bfloat16):
    result = spread * jax.random.normal(rng, extent, jnp.float32)
    if cuts:
        result = result * levels(rng, extent, cuts, -0.22, 0.18)
    return jnp.clip(result, -limit, limit).astype(held_as)


def setup_inputs(seed: int = 0) -> dict:
    arg_keys = jax.random.split(jax.random.key(seed), 9)
    return {
        "frames_x": draw_frames_x(jax.random.fold_in(arg_keys[8], 71), 0),
        "box_embed": scatter_about(arg_keys[1], (NV, FRAMES, NB, D), 1.0, 6.0, ((0, 8), (1, 64))),
        "box_count": with_ends(jax.random.randint(arg_keys[2], (NV, FRAMES), 1, NB + 1), jax.random.fold_in(arg_keys[2], 1), 1, NB).astype(jnp.int32),
        "frame_valid": with_ends((jax.random.randint(arg_keys[3], (NV, FRAMES), 0, 4) < 3).astype(jnp.int32), jax.random.fold_in(arg_keys[3], 1), 0, 1),
        "cycle_link": with_ends((jax.random.randint(arg_keys[4], (NV, 2), 0, 4) < 3).astype(jnp.int32), jax.random.fold_in(arg_keys[4], 1), 0, 1),
        "w_qkv": draw_w_qkv(jax.random.fold_in(arg_keys[8], 71), 0),
        "w_out": scatter_about(arg_keys[6], (D, D), D ** -0.5, 0.1875, ((0, 64),)),
        "box_gate": jnp.clip(jax.random.uniform(arg_keys[7], (BOX_HEADS * HD,), jnp.float32, -2.0, 2.0), -2.0, 2.0),
    }


def attend(queries, key_rows, value_rows, live_mask):
    scale = HD ** -0.5
    scores = jnp.einsum("qhe,khe->hqk", queries.astype(jnp.float32), key_rows.astype(jnp.float32)) * scale
    scores = jnp.where(live_mask[None, None, :] > 0, scores, -1e30)
    row_max = jnp.max(scores, axis=-1, keepdims=True)
    expos = jnp.exp(scores - row_max)
    weights = (expos / jnp.sum(expos, axis=-1, keepdims=True)).astype(jnp.bfloat16)
    return jnp.einsum("hqk,khe->qhe", weights.astype(jnp.float32), value_rows.astype(jnp.float32))


def reference(frames_x, box_embed, box_count, frame_valid, cycle_link, w_qkv, w_out, box_gate):
    cross_width = CROSS_HEADS * HD
    time_width = TIME_HEADS * HD
    box_width = BOX_HEADS * HD

    def project(camera):
        token_rows = camera.reshape(FRAMES * P_SIZE, D)
        product = jnp.dot(token_rows, w_qkv, preferred_element_type=jnp.float32)
        return product.astype(jnp.bfloat16).reshape(FRAMES, P_SIZE, 3 * D)

    qkv = lax.map(project, frames_x)
    box_columns = jnp.concatenate([w_qkv[:, 2 * D - box_width:2 * D], w_qkv[:, 3 * D - box_width:]], axis=1)
    box_kv = jnp.dot(box_embed.reshape(NV * FRAMES * NB, D), box_columns, preferred_element_type=jnp.float32)
    box_kv = box_kv.astype(jnp.bfloat16).reshape(NV, FRAMES * NB, 2 * box_width)
    slot_ids = jnp.arange(NB, dtype=jnp.int32)
    box_live = ((slot_ids[None, None, :] < box_count[:, :, None]) & (frame_valid[:, :, None] == 1))
    box_live = box_live.astype(jnp.float32).reshape(NV, FRAMES * NB)
    cross_keys = qkv[..., D:D + cross_width]
    cross_values = qkv[..., 2 * D:2 * D + cross_width]
    keys_all = jnp.concatenate([jnp.roll(cross_keys, 1, 0), cross_keys, jnp.roll(cross_keys, -1, 0)], axis=2)
    values_all = jnp.concatenate([jnp.roll(cross_values, 1, 0), cross_values, jnp.roll(cross_values, -1, 0)], axis=2)
    all_ones = jnp.ones((P_SIZE,), jnp.float32)
    frame_ones = jnp.ones((FRAMES,), jnp.float32)

    def camera_block(camera_index):
        link_flags = cycle_link[camera_index].astype(jnp.float32)
        cross_live = jnp.concatenate([all_ones * link_flags[0], all_ones, all_ones * link_flags[1]])
        camera_qkv = qkv[camera_index]
        camera_box = box_kv[camera_index]
        box_mask = jnp.concatenate([all_ones, box_live[camera_index]])

        def frame_block(frame_index):
            frame_row = camera_qkv[frame_index]
            cross_query = frame_row[:, :cross_width].reshape(P_SIZE, CROSS_HEADS, HD)
            cross_key = keys_all[camera_index, frame_index].reshape(3 * P_SIZE, CROSS_HEADS, HD)
            cross_value = values_all[camera_index, frame_index].reshape(3 * P_SIZE, CROSS_HEADS, HD)
            cross = attend(cross_query, cross_key, cross_value, cross_live).reshape(P_SIZE, cross_width)
            box_query = frame_row[:, cross_width + time_width:D].reshape(P_SIZE, BOX_HEADS, HD)
            box_key = jnp.concatenate([frame_row[:, 2 * D - box_width:2 * D], camera_box[:, :box_width]], axis=0)
            box_value = jnp.concatenate([frame_row[:, 3 * D - box_width:], camera_box[:, box_width:]], axis=0)
            boxed = attend(box_query, box_key.reshape(-1, BOX_HEADS, HD), box_value.reshape(-1, BOX_HEADS, HD), box_mask)
            boxed = boxed.reshape(P_SIZE, box_width) * jnp.tanh(box_gate)
            return cross, boxed

        cross, boxed = lax.map(frame_block, jnp.arange(FRAMES, dtype=jnp.int32))
        time_query = camera_qkv[..., cross_width:cross_width + time_width].reshape(FRAMES, P_SIZE, TIME_HEADS, HD)
        time_key = camera_qkv[..., D + cross_width:D + cross_width + time_width].reshape(FRAMES, P_SIZE, TIME_HEADS, HD)
        time_value = camera_qkv[..., 2 * D + cross_width:2 * D + cross_width + time_width].reshape(FRAMES, P_SIZE, TIME_HEADS, HD)
        timed = jax.vmap(lambda qq, kk, vv: attend(qq, kk, vv, frame_ones), in_axes=1, out_axes=1)(time_query, time_key, time_value)
        attn = jnp.concatenate([cross, timed.reshape(FRAMES, P_SIZE, time_width), boxed], axis=-1).astype(jnp.bfloat16)
        projected = jnp.dot(attn.reshape(FRAMES * P_SIZE, D), w_out, preferred_element_type=jnp.float32)
        residual = frames_x[camera_index].reshape(FRAMES * P_SIZE, D).astype(jnp.float32)
        return (residual + projected).astype(jnp.bfloat16).reshape(FRAMES, P_SIZE, D)

    return lax.map(camera_block, jnp.arange(NV, dtype=jnp.int32))
```

```python
import functools

import jax
import jax.numpy as jnp
from jax import lax
from jax.experimental import pallas as pl
from jax.experimental.pallas import tpu as pltpu
from jax.sharding import PartitionSpec as P

MESH = pl.DeviceIdType.MESH
XC = 640
ZQ = 896
ZW = 2048
QX = 4 * XC
HD = 72
CROSS_HEADS = 8
TIME_HEADS = 4
BOX_HEADS = 4


def gather_kernel(wq, wo, xin, wx, wz, xn, m, stage, ssem, msem, rxs, rzs, nsem, lsem):
    v = lax.axis_index("view")
    t = lax.axis_index("tm")
    core = lax.rem(v, 2)
    x = lax.rem(t, 4)
    z = lax.rem(t // 4, 8)
    yh = t // 32
    up, down = lax.rem(v + 1, 8), lax.rem(v + 7, 8)
    partner = v + 1 - 2 * core
    d = 1 - 2 * core

    def tm(yy, zz, xx):
        return (yy * 8 + zz) * 4 + xx

    def zat(k):
        return lax.rem(z + d * k + 16, 8)

    barrier = pltpu.get_barrier_semaphore()
    peers = [(up, t), (down, t)]
    peers += [(v, tm(yh, z, lax.rem(x + j, 4))) for j in range(1, 4)]
    peers += [(v, tm(1 - yh, z, lax.rem(x + j, 4))) for j in range(4)]
    peers += [(v, tm(yh, zat(1), x)), (v, tm(yh, zat(-1), x))]
    for p in peers:
        pl.semaphore_signal(barrier, inc=1, device_id=p, device_id_type=MESH)
    pl.semaphore_wait(barrier, len(peers))

    sends = []

    def send(src, dst, rsem, to):
        c = pltpu.make_async_remote_copy(
            src_ref=src,
            dst_ref=dst,
            send_sem=ssem.at[len(sends)],
            recv_sem=rsem,
            device_id=to,
            device_id_type=MESH,
        )
        c.start()
        sends.append(c)

    def arrived(ref, sem):
        pltpu.make_async_copy(ref, ref, sem).wait()

    @pl.when(core == yh)
    def _():
        def pieces(xx):
            cols = pl.ds(pl.multiple_of(xx * XC, 128), XC)
            return [
                (wq.at[:, cols], m.at[x, :, pl.ds(0, XC)], 0),
                (wq.at[:, pl.ds(QX, ZQ)], m.at[x, :, pl.ds(XC, ZQ)], 1),
                (wo, m.at[x, :, pl.ds(XC + ZQ, ZW - ZQ)], 2),
            ]

        out, own = [], []
        for yy, js in ((0, range(4)), (1, range(4))):
            for j in js:
                xx = lax.rem(x + j, 4)
                far = lax.rem(yh + yy, 2)
                for src, dst, k in pieces(xx):
                    if yy == 0 and j == 0:
                        c = pltpu.make_async_copy(src, dst, msem.at[x, k])
                        c.start()
                    else:
                        c = pltpu.make_async_remote_copy(
                            src_ref=src,
                            dst_ref=dst,
                            send_sem=lsem.at[len(out)],
                            recv_sem=msem.at[x, k],
                            device_id=(v, tm(far, z, xx)),
                            device_id_type=MESH,
                        )
                        c.start()
                        out.append(c)
        for c in out:
            c.wait_send()

    send(xin, xn.at[0], nsem.at[0], (up, t))
    send(xin, xn.at[1], nsem.at[1], (down, t))

    row = lax.broadcasted_iota(jnp.int32, (72, 18), 0)
    col = lax.broadcasted_iota(jnp.int32, (72, 18), 1)
    for xx in range(4):
        arrived(m.at[xx, :, pl.ds(0, XC)], msem.at[xx, 0])
        arrived(m.at[xx, :, pl.ds(XC, ZQ)], msem.at[xx, 1])
        arrived(m.at[xx, :, pl.ds(XC + ZQ, ZW - ZQ)], msem.at[xx, 2])
    acc = jnp.zeros((72, XC + ZW), jnp.float32)
    for xx in range(4):
        pick = (row == col + 18 * xx).astype(jnp.bfloat16)
        acc += jnp.dot(pick, m[xx], preferred_element_type=jnp.float32)
    stage[...] = acc.astype(jnp.bfloat16)

    mine = core * 8
    b0 = mine + z
    own = [
        pltpu.make_async_copy(stage.at[:, pl.ds(0, XC)], wx.at[x, b0], rxs.at[x, b0]),
        pltpu.make_async_copy(stage.at[:, pl.ds(XC, ZW)], wz.at[b0], rzs.at[b0]),
    ]
    for c in own:
        c.start()

    def spread(b, srcx, srcz, nxt):
        for n in nxt:
            send(srcx, wx.at[x, b], rxs.at[x, b], (v, tm(yh, n, x)))
            send(srcz, wz.at[b], rzs.at[b], (v, tm(yh, n, x)))
        for j in (1, 3, 2):
            send(srcx, wx.at[x, b], rxs.at[x, b], (v, tm(yh, z, lax.rem(x + j, 4))))
        send(srcx, wx.at[x, b], rxs.at[x, b], (partner, t))
        send(srcz, wz.at[b], rzs.at[b], (partner, t))

    def relay(b):
        for j in (1, 3, 2):
            xx = lax.rem(x + j, 4)
            arrived(wx.at[xx, b], rxs.at[xx, b])
            send(wx.at[xx, b], wx.at[xx, b], rxs.at[xx, b], (partner, t))

    spread(b0, stage.at[:, pl.ds(0, XC)], stage.at[:, pl.ds(XC, ZW)], (zat(1), zat(-1)))
    todo = [b0]
    for s in range(1, 5):
        for sign in (1, -1):
            if sign < 0 and s == 4:
                continue
            b = mine + zat(-s * sign)
            arrived(wx.at[x, b], rxs.at[x, b])
            arrived(wz.at[b], rzs.at[b])
            last = s == 4 or (sign < 0 and s == 3)
            spread(b, wx.at[x, b], wz.at[b], () if last else (zat(sign),))
            todo.append(b)
        if s > 1:
            relay(todo.pop(0))
    for b in todo:
        relay(b)
    for c in own:
        c.wait()
    other = 8 - mine
    for k in range(8):
        b = other + k
        arrived(wz.at[b], rzs.at[b])
        for xx in range(4):
            arrived(wx.at[xx, b], rxs.at[xx, b])
    arrived(xn.at[0], nsem.at[0])
    arrived(xn.at[1], nsem.at[1])
    for c in sends:
        c.wait_send()


def gather(w_qkv, w_out, rows):
    hbm = pl.BlockSpec(memory_space=pl.ANY)
    bf = jnp.bfloat16
    return pl.pallas_call(
        gather_kernel,
        out_shape=(
            jax.ShapeDtypeStruct((4, 16, 72, XC), bf),
            jax.ShapeDtypeStruct((16, 72, ZW), bf),
            jax.ShapeDtypeStruct((2,) + rows.shape, bf),
        ),
        in_specs=[hbm] * 3,
        out_specs=(hbm,) * 3,
        scratch_shapes=[
            pltpu.VMEM((4, 18, XC + ZW), bf),
            pltpu.VMEM((72, XC + ZW), bf),
            pltpu.SemaphoreType.DMA((90,)),
            pltpu.SemaphoreType.DMA((4, 3)),
            pltpu.SemaphoreType.DMA((4, 16)),
            pltpu.SemaphoreType.DMA((16,)),
            pltpu.SemaphoreType.DMA((2,)),
            pltpu.SemaphoreType.DMA((21,)),
        ],
        compiler_params=pltpu.CompilerParams(collective_id=0, has_side_effects=True),
        name="gather",
    )(w_qkv, w_out, rows)


def side_by_side_2(arrays, axis, dim, along):
    columns = [a.reshape(*a.shape[:along], -1) for a in arrays]
    both = jnp.concatenate(columns, axis=along)
    out, at, done = (lax.all_gather(both, axis, axis=dim, tiled=True), 0, [])
    for a, column in zip(arrays, columns):
        share = out[..., at : at + column.shape[along]]
        done.append(share.reshape(*share.shape[:along], *a.shape[along:]))
        at += column.shape[along]
    return tuple(done)


def padded_2(cells, sides, width):
    for axis, dim in sides:
        count = lax.axis_size(axis)
        head = lax.slice_in_dim(cells, 0, width, axis=dim)
        tail = lax.slice_in_dim(cells, cells.shape[dim] - width, cells.shape[dim], axis=dim)
        cells = jnp.concatenate(
            [
                lax.ppermute(tail, axis, [(i, (i + 1) % count) for i in range(count)]),
                cells,
                lax.ppermute(head, axis, [((i + 1) % count, i) for i in range(count)]),
            ],
            axis=dim,
        )
    return cells


def sent_together(arrays, axis, split_dim, concat_dim, along):
    both = jnp.concatenate(arrays, axis=along)
    out, at, done = (
        lax.all_to_all(both, axis, split_axis=split_dim, concat_axis=concat_dim, tiled=True),
        0,
        [],
    )
    for a in arrays:
        done.append(lax.slice_in_dim(out, at, at + a.shape[along], axis=along))
        at += a.shape[along]
    return tuple(done)


def in_blocks(value, dim, devices):
    before, after = (value.shape[:dim], value.shape[dim + 1 :])
    return jnp.moveaxis(value.reshape(*before, devices, -1, *after), dim, 0)


def piece_ends(length, count):
    turn = length // count
    if turn >= 8:
        turn -= turn % 8
    return [turn * k for k in range(1, count)]


def in_order(tiles, dim):
    lengths = list(tiles.shape[1:])
    lengths[dim] *= tiles.shape[0]
    return jnp.moveaxis(tiles, 0, dim).reshape(lengths)


def exchange_in_pieces(value, axis, pieces, split_dim, concat_dim):
    tiles = in_blocks(value, split_dim, lax.axis_size(axis))
    cut = max(range(1, max(2, tiles.ndim - 1)), key=lambda d: tiles.shape[d])
    done = []
    for share in jnp.split(tiles, piece_ends(tiles.shape[cut], pieces), axis=cut):
        if share.size:
            done.append(lax.all_to_all(share, axis, split_axis=0, concat_axis=0, tiled=True))
    return in_order(jnp.concatenate(done, axis=cut), concat_dim)


def attend(queries, key_rows, value_rows, live_mask):
    scale = HD ** (-0.5)
    scores = (
        jnp.einsum("qhe,khe->hqk", queries, key_rows, preferred_element_type=jnp.float32) * scale
    )
    scores = jnp.where(live_mask[None, None, :] > 0, scores, -1e30)
    row_max = jnp.max(scores, axis=-1, keepdims=True)
    expos = jnp.exp(scores - row_max)
    weights = (expos / jnp.sum(expos, axis=-1, keepdims=True)).astype(jnp.bfloat16)
    return jnp.einsum("hqk,khe->qhe", weights, value_rows, preferred_element_type=jnp.float32)


def box_columns(matrix):
    model_width = matrix.shape[1] // 3
    box_width = BOX_HEADS * HD
    return jnp.concatenate(
        [
            matrix[:, 2 * model_width - box_width : 2 * model_width],
            matrix[:, 3 * model_width - box_width :],
        ],
        axis=1,
    )


def per_device(frames_x, box_embed, box_count, frame_valid, cycle_link, w_qkv, w_out, box_gate):
    model_width = frames_x.shape[3]
    frame_count = frames_x.shape[1]
    token_count = frames_x.shape[2]
    slot_count = box_embed.shape[2]
    cross_width = CROSS_HEADS * HD
    time_width = TIME_HEADS * HD
    box_width = BOX_HEADS * HD
    token_rows = frames_x.reshape(frame_count * token_count, model_width)
    slot_ids = lax.broadcasted_iota(jnp.int32, (frame_count, slot_count), 1)
    live_own = (slot_ids < box_count[0][:, None]) & (frame_valid[0][:, None] == 1)
    live_own = live_own.astype(jnp.bfloat16).reshape(frame_count * slot_count)
    box_rows = box_embed.reshape(frame_count * slot_count, model_width)
    wx, wz, _ = gather(w_qkv, w_out, token_rows)
    wx = wx.reshape(4, model_width, XC)
    wz = wz.reshape(model_width, ZW)
    whole_qkv = jnp.concatenate([wx[0], wx[1], wx[2], wx[3], wz[:, :ZQ]], axis=1)
    whole_out = wz[:, ZQ:]
    qkv = jnp.dot(token_rows, whole_qkv, preferred_element_type=jnp.float32).astype(jnp.bfloat16)
    box_kv = jnp.dot(box_rows, box_columns(whole_qkv), preferred_element_type=jnp.float32).astype(
        jnp.bfloat16
    )
    box_kv, box_live = side_by_side_2((box_kv, live_own), "tm", 0, 1)
    qkv = qkv.reshape(frame_count, token_count, 3 * model_width)
    cross_keys = qkv[..., model_width : model_width + cross_width]
    cross_values = qkv[..., 2 * model_width : 2 * model_width + cross_width]
    stacked = jnp.stack([cross_keys, cross_values])[:, None]
    padded = padded_2(stacked, (("view", 1),), 1)
    prev_keys, prev_values = (padded[0, 0], padded[1, 0])
    next_keys, next_values = (padded[0, 2], padded[1, 2])
    keys_all = jnp.concatenate([prev_keys, cross_keys, next_keys], axis=1)
    values_all = jnp.concatenate([prev_values, cross_values, next_values], axis=1)
    time_query = qkv[..., cross_width : cross_width + time_width]
    time_key = qkv[..., model_width + cross_width : model_width + cross_width + time_width]
    time_value = qkv[
        ..., 2 * model_width + cross_width : 2 * model_width + cross_width + time_width
    ]
    query_all, key_all, value_all = sent_together((time_query, time_key, time_value), "tm", 1, 0, 2)
    total_frames = query_all.shape[0]
    position_count = query_all.shape[1]
    frame_ones = jnp.ones((total_frames,), jnp.float32)
    timed = jax.vmap(lambda qq, kk, vv: attend(qq, kk, vv, frame_ones), in_axes=1, out_axes=1)(
        query_all.reshape(total_frames, position_count, TIME_HEADS, HD),
        key_all.reshape(total_frames, position_count, TIME_HEADS, HD),
        value_all.reshape(total_frames, position_count, TIME_HEADS, HD),
    )
    timed = timed.reshape(total_frames, position_count, time_width).astype(jnp.bfloat16)
    timed = exchange_in_pieces(timed, "tm", 2, 0, 1)
    all_ones = jnp.ones((token_count,), jnp.float32)
    link_flags = cycle_link[0].astype(jnp.float32)
    cross_live = jnp.concatenate([all_ones * link_flags[0], all_ones, all_ones * link_flags[1]])
    box_mask = jnp.concatenate([all_ones, box_live.astype(jnp.float32)])
    gate_factor = jnp.tanh(box_gate)

    def frame_block(frame_index):
        frame_row = qkv[frame_index]
        cross_query = frame_row[:, :cross_width].reshape(token_count, CROSS_HEADS, HD)
        cross_key = keys_all[frame_index].reshape(3 * token_count, CROSS_HEADS, HD)
        cross_value = values_all[frame_index].reshape(3 * token_count, CROSS_HEADS, HD)
        cross = attend(cross_query, cross_key, cross_value, cross_live).reshape(
            token_count, cross_width
        )
        box_query = frame_row[:, cross_width + time_width : model_width].reshape(
            token_count, BOX_HEADS, HD
        )
        box_key = jnp.concatenate(
            [frame_row[:, 2 * model_width - box_width : 2 * model_width], box_kv[:, :box_width]],
            axis=0,
        )
        box_value = jnp.concatenate(
            [frame_row[:, 3 * model_width - box_width :], box_kv[:, box_width:]], axis=0
        )
        boxed = attend(
            box_query,
            box_key.reshape(-1, BOX_HEADS, HD),
            box_value.reshape(-1, BOX_HEADS, HD),
            box_mask,
        )
        boxed = boxed.reshape(token_count, box_width) * gate_factor
        return (cross, boxed)

    cross, boxed = lax.map(frame_block, jnp.arange(frame_count, dtype=jnp.int32))
    attn = jnp.concatenate([cross, timed.astype(jnp.float32), boxed], axis=-1).astype(jnp.bfloat16)
    flat_attn = attn.reshape(frame_count * token_count, model_width)
    projected = jnp.dot(flat_attn, whole_out, preferred_element_type=jnp.float32)
    result = (token_rows.astype(jnp.float32) + projected).astype(jnp.bfloat16)
    return result.reshape(frames_x.shape)


def solution(mesh):
    in_specs = (
        P("view", "tm", None, None),
        P("view", "tm", None, None),
        P("view", "tm"),
        P("view", "tm"),
        P("view", None),
        P("tm", None),
        P("tm", None),
        P(),
    )
    out_specs = P("view", "tm", None, None)
    return jax.shard_map(
        per_device, mesh=mesh, in_specs=in_specs, out_specs=out_specs, check_vma=False
    )
```

```python
import jax
import jax.numpy as jnp
from jax import lax
from jax.experimental import pallas as pl
from jax.experimental.pallas import tpu as pltpu
from jax.sharding import PartitionSpec as P

MESH = pl.DeviceIdType.MESH
XC = 640
ZQ = 896
ZW = 2048
QX = 4 * XC
D = 1152
TOKENS = 384
HD = 72
CROSS_HEADS = 8
TIME_HEADS = 4
BOX_HEADS = 4
NEG = -1e30
EXP_SCALE = HD**-0.5 * 1.4426950408889634


def gather_kernel(wq, wo, xin, wx, wz, xn, m, stage, ssem, msem, rxs, rzs, nsem, lsem):
    v = lax.axis_index("view")
    t = lax.axis_index("tm")
    core = lax.rem(v, 2)
    x = lax.rem(t, 4)
    z = lax.rem(t // 4, 8)
    yh = t // 32
    up, down = lax.rem(v + 1, 8), lax.rem(v + 7, 8)
    partner = v + 1 - 2 * core
    d = 1 - 2 * core

    def tm(yy, zz, xx):
        return (yy * 8 + zz) * 4 + xx

    def zat(k):
        return lax.rem(z + d * k + 16, 8)

    barrier = pltpu.get_barrier_semaphore()
    peers = [(up, t), (down, t)]
    peers += [(v, tm(yh, z, lax.rem(x + j, 4))) for j in range(1, 4)]
    peers += [(v, tm(1 - yh, z, lax.rem(x + j, 4))) for j in range(4)]
    peers += [(v, tm(yh, zat(1), x)), (v, tm(yh, zat(-1), x))]
    for p in peers:
        pl.semaphore_signal(barrier, inc=1, device_id=p, device_id_type=MESH)
    pl.semaphore_wait(barrier, len(peers))

    sends = []

    def send(src, dst, rsem, to):
        c = pltpu.make_async_remote_copy(
            src_ref=src,
            dst_ref=dst,
            send_sem=ssem.at[len(sends)],
            recv_sem=rsem,
            device_id=to,
            device_id_type=MESH,
        )
        c.start()
        sends.append(c)

    def arrived(ref, sem):
        pltpu.make_async_copy(ref, ref, sem).wait()

    @pl.when(core == yh)
    def _():
        def pieces(xx):
            cols = pl.ds(pl.multiple_of(xx * XC, 128), XC)
            return [
                (wq.at[:, cols], m.at[x, :, pl.ds(0, XC)], 0),
                (wq.at[:, pl.ds(QX, ZQ)], m.at[x, :, pl.ds(XC, ZQ)], 1),
                (wo, m.at[x, :, pl.ds(XC + ZQ, ZW - ZQ)], 2),
            ]

        out, own = [], []
        for yy, js in ((0, range(4)), (1, range(4))):
            for j in js:
                xx = lax.rem(x + j, 4)
                far = lax.rem(yh + yy, 2)
                for src, dst, k in pieces(xx):
                    if yy == 0 and j == 0:
                        c = pltpu.make_async_copy(src, dst, msem.at[x, k])
                        c.start()
                    else:
                        c = pltpu.make_async_remote_copy(
                            src_ref=src,
                            dst_ref=dst,
                            send_sem=lsem.at[len(out)],
                            recv_sem=msem.at[x, k],
                            device_id=(v, tm(far, z, xx)),
                            device_id_type=MESH,
                        )
                        c.start()
                        out.append(c)
        for c in out:
            c.wait_send()

    send(xin, xn.at[0], nsem.at[0], (up, t))
    send(xin, xn.at[1], nsem.at[1], (down, t))

    row = lax.broadcasted_iota(jnp.int32, (72, 18), 0)
    col = lax.broadcasted_iota(jnp.int32, (72, 18), 1)
    for xx in range(4):
        arrived(m.at[xx, :, pl.ds(0, XC)], msem.at[xx, 0])
        arrived(m.at[xx, :, pl.ds(XC, ZQ)], msem.at[xx, 1])
        arrived(m.at[xx, :, pl.ds(XC + ZQ, ZW - ZQ)], msem.at[xx, 2])
    acc = jnp.zeros((72, XC + ZW), jnp.float32)
    for xx in range(4):
        pick = (row == col + 18 * xx).astype(jnp.bfloat16)
        acc += jnp.dot(pick, m[xx], preferred_element_type=jnp.float32)
    stage[...] = acc.astype(jnp.bfloat16)

    mine = core * 8
    b0 = mine + z
    own = [
        pltpu.make_async_copy(stage.at[:, pl.ds(0, XC)], wx.at[x, b0], rxs.at[x, b0]),
        pltpu.make_async_copy(stage.at[:, pl.ds(XC, ZW)], wz.at[b0], rzs.at[b0]),
    ]
    for c in own:
        c.start()

    def spread(b, srcx, srcz, nxt):
        for n in nxt:
            send(srcx, wx.at[x, b], rxs.at[x, b], (v, tm(yh, n, x)))
            send(srcz, wz.at[b], rzs.at[b], (v, tm(yh, n, x)))
        for j in (1, 3, 2):
            send(srcx, wx.at[x, b], rxs.at[x, b], (v, tm(yh, z, lax.rem(x + j, 4))))
        send(srcx, wx.at[x, b], rxs.at[x, b], (partner, t))
        send(srcz, wz.at[b], rzs.at[b], (partner, t))

    def relay(b):
        for j in (1, 3, 2):
            xx = lax.rem(x + j, 4)
            arrived(wx.at[xx, b], rxs.at[xx, b])
            send(wx.at[xx, b], wx.at[xx, b], rxs.at[xx, b], (partner, t))

    spread(b0, stage.at[:, pl.ds(0, XC)], stage.at[:, pl.ds(XC, ZW)], (zat(1), zat(-1)))
    todo = [b0]
    for s in range(1, 5):
        for sign in (1, -1):
            if sign < 0 and s == 4:
                continue
            b = mine + zat(-s * sign)
            arrived(wx.at[x, b], rxs.at[x, b])
            arrived(wz.at[b], rzs.at[b])
            last = s == 4 or (sign < 0 and s == 3)
            spread(b, wx.at[x, b], wz.at[b], () if last else (zat(sign),))
            todo.append(b)
        if s > 1:
            relay(todo.pop(0))
    for b in todo:
        relay(b)
    for c in own:
        c.wait()
    other = 8 - mine
    for k in range(8):
        b = other + k
        arrived(wz.at[b], rzs.at[b])
        for xx in range(4):
            arrived(wx.at[xx, b], rxs.at[xx, b])
    arrived(xn.at[0], nsem.at[0])
    arrived(xn.at[1], nsem.at[1])
    for c in sends:
        c.wait_send()


def gather(w_qkv, w_out, rows):
    hbm = pl.BlockSpec(memory_space=pl.ANY)
    bf = jnp.bfloat16
    return pl.pallas_call(
        gather_kernel,
        out_shape=(
            jax.ShapeDtypeStruct((4, 16, 72, XC), bf),
            jax.ShapeDtypeStruct((16, 72, ZW), bf),
            jax.ShapeDtypeStruct((2,) + rows.shape, bf),
        ),
        in_specs=[hbm] * 3,
        out_specs=(hbm,) * 3,
        scratch_shapes=[
            pltpu.VMEM((4, 18, XC + ZW), bf),
            pltpu.VMEM((72, XC + ZW), bf),
            pltpu.SemaphoreType.DMA((90,)),
            pltpu.SemaphoreType.DMA((4, 3)),
            pltpu.SemaphoreType.DMA((4, 16)),
            pltpu.SemaphoreType.DMA((16,)),
            pltpu.SemaphoreType.DMA((2,)),
            pltpu.SemaphoreType.DMA((21,)),
        ],
        compiler_params=pltpu.CompilerParams(collective_id=0, has_side_effects=True),
        name="gather",
    )(w_qkv, w_out, rows)


def attend_kernel(
    x_ref, xn_ref, wx_ref, wz_ref, box_ref, cnt_ref, val_ref, link_ref, gate_ref, out_ref,
    qkv, nbr, tsend, tqkv, tout, timed, kvb, bkv, qc, kc, vc, qb, kb, vb, oh,
    ts_send, ts_recv, to_send, to_recv, ba_send, ba_recv, br_send, br_recv, own_sem,
):
    bf, f32 = jnp.bfloat16, jnp.float32
    v = lax.axis_index("view")
    t = lax.axis_index("tm")
    core = lax.rem(v, 2)
    x = lax.rem(t, 4)
    z = lax.rem(t // 4, 8)
    yh = t // 32
    d = 1 - 2 * core
    v4 = lax.rem(v + 4, 8)
    owner = (t // 4) * 3 + x
    base = (t * 3) // 4

    def tm(yy, zz, xx):
        return (yy * 8 + zz) * 4 + xx

    def zat(k):
        return lax.rem(z + d * k + 16, 8)

    plane = [tm(yh, z, lax.rem(x + j, 4)) for j in range(1, 4)]
    plane += [tm(1 - yh, z, lax.rem(x + j, 4)) for j in range(4)]
    barrier = pltpu.get_barrier_semaphore()

    @pl.loop(0, 64)
    def _(i):
        pl.semaphore_signal(barrier, inc=1, device_id=(v4, i), device_id_type=MESH)

    for p in plane + [tm(yh, zat(1), x), tm(yh, zat(-1), x)]:
        pl.semaphore_signal(barrier, inc=1, device_id=(v, p), device_id_type=MESH)

    def mm(a, b):
        return jnp.dot(a, b, preferred_element_type=f32)

    rows = x_ref[...]
    for i in range(4):
        qkv[:, i * XC : (i + 1) * XC] = mm(rows, wx_ref[i])
    qkv[:, QX : QX + ZQ] = mm(rows, wz_ref[:, :ZQ])

    tq = [qkv[:, c * 128 : c * 128 + 896] for c in (4, 13)]
    tq.append(jnp.concatenate([qkv[:, 2816:3456], qkv[:, 0:256]], axis=1))
    lane = lax.broadcasted_iota(jnp.int32, (TOKENS, 896), 1)
    packed = pltpu.roll(tq[0], 896 - 64, 1)
    packed = jnp.where(lane < 288, packed, pltpu.roll(tq[1], 288 - 64, 1))
    packed = jnp.where(lane < 576, packed, pltpu.roll(tq[2], 576 - 64, 1))
    tsend[...] = packed.astype(bf).reshape(48, 8, 896)

    boxes = box_ref[...]
    bv = jnp.concatenate([mm(boxes, wx_ref[3][:, 0:384]), mm(boxes, wz_ref[:, 512:896])], axis=1)
    slot = lax.broadcasted_iota(jnp.int32, (16, 768), 0)
    blane = lax.broadcasted_iota(jnp.int32, (16, 768), 1)
    live = jnp.logical_and(slot < cnt_ref[0, 0], val_ref[0, 0] == 1)
    bv = jnp.where(blane == 0, jnp.where(live, 0.0, NEG), bv)
    kvb[...] = bv.astype(bf)

    pl.semaphore_wait(barrier, 73)

    def time_copy(i):
        o = lax.rem(i + base, 48)
        return pltpu.make_async_remote_copy(
            src_ref=tsend.at[o],
            dst_ref=tqkv.at[t],
            send_sem=ts_send.at[i],
            recv_sem=ts_recv.at[t],
            device_id=(v4, (o // 3) * 4 + lax.rem(o, 3)),
            device_id_type=MESH,
        )

    @pl.loop(0, 48)
    def _(i):
        time_copy(i).start()

    own = pltpu.make_async_copy(kvb, bkv.at[t], own_sem)
    own.start()
    first = []
    for k, p in enumerate(plane):
        c = pltpu.make_async_remote_copy(
            src_ref=kvb,
            dst_ref=bkv.at[t],
            send_sem=ba_send.at[k],
            recv_sem=ba_recv.at[yh * 4 + x],
            device_id=(v, p),
            device_id_type=MESH,
        )
        c.start()
        first.append(c)

    near = xn_ref[...].reshape(2 * TOKENS, D)
    nbr[:, 0:128] = mm(near, wx_ref[1][:, 512:640])
    nbr[:, 128:640] = mm(near, wx_ref[2][:, 0:512])
    nbr[:, 640:896] = mm(near, wx_ref[3][:, 384:640])
    nbr[:, 896:1280] = mm(near, wz_ref[:, 0:384])

    def tile(a, off, fill):
        piece = pltpu.roll(a, (a.shape[1] - off) % a.shape[1], 1)[:, :128] if off else a[:, :128]
        at = lax.broadcasted_iota(jnp.int32, piece.shape, 1)
        return jnp.where(at < HD, piece, jnp.where(at == HD, fill, 0.0)).astype(bf)

    def head(ref, r0, r1, c, fill):
        lo = c // 128 * 128
        a = ref[r0:r1, lo : min(lo + 256, ref.shape[1])]
        return tile(a, c - lo, fill)

    gone = [jnp.where(link_ref[0, i] > 0, 0.0, NEG) for i in range(2)]
    n = TOKENS
    for h in range(CROSS_HEADS):
        qc[h] = head(qkv, 0, n, HD * h, 1.0)
        for s, (ref, r0, ck, cv, fill) in enumerate(
            (
                (nbr, 0, 0, 640, gone[0]),
                (qkv, 0, D, 2 * D, 0.0),
                (nbr, n, 0, 640, gone[1]),
            )
        ):
            kc[h, s * n : (s + 1) * n] = head(ref, r0, r0 + n, ck + HD * h, fill)
            vc[h, s * n : (s + 1) * n] = head(ref, r0, r0 + n, cv + HD * h, 1.0)
    at0 = (CROSS_HEADS + TIME_HEADS) * HD
    for h in range(BOX_HEADS):
        qb[h] = head(qkv, 0, n, at0 + HD * h, 1.0)
        kb[h, 0:n] = head(qkv, 0, n, D + at0 + HD * h, 0.0)
        vb[h, 0:n] = head(qkv, 0, n, 2 * D + at0 + HD * h, 1.0)

    own.wait()
    for yy in range(2):
        for j in range(4):
            xx = lax.rem(x + j, 4)

            def take(yy=yy, xx=xx):
                ref = bkv.at[tm(lax.rem(yh + yy, 2), z, xx)]
                pltpu.make_async_copy(ref, ref, ba_recv.at[lax.rem(yh + yy, 2) * 4 + xx]).wait()

            if yy or j:
                take()

    def group(yy, zz):
        return bkv.at[pl.ds(tm(yy, zz, 0), 4)]

    def ring(yy, zz, to, k):
        return pltpu.make_async_remote_copy(
            src_ref=group(yy, zz),
            dst_ref=group(yy, zz),
            send_sem=br_send.at[k],
            recv_sem=br_recv.at[yy * 8 + zz],
            device_id=(v, tm(yh, to, x)),
            device_id_type=MESH,
        )

    sent = []

    def start(c):
        c.start()
        sent.append(c)

    for yy in range(2):
        for sign in (1, -1):
            start(ring(yy, z, zat(sign), len(sent)))

    def relay(s):
        for sign in (1, -1):
            if sign < 0 and s == 4:
                continue
            zz = zat(-s * sign)
            for yy in range(2):
                ref = group(yy, zz)
                pltpu.make_async_copy(ref, ref, br_recv.at[yy * 8 + zz]).wait()
                if s < (4 if sign > 0 else 3):
                    start(ring(yy, zz, zat(sign), len(sent)))

    def softmax_dot(q, k, val):
        s = lax.dot_general(q, k, (((1,), (1,)), ((), ())), preferred_element_type=f32)
        top = jnp.max(s, axis=1, keepdims=True)
        p = jnp.exp2((s - top) * EXP_SCALE).astype(bf)
        return mm(p, val)

    def heads(first_head, count, q_ref, k_ref, v_ref, out0):
        @pl.loop(first_head, first_head + count)
        def _(h):
            for r in range(0, n, 128):
                o = softmax_dot(q_ref[h, r : r + 128], k_ref[h], v_ref[h])
                oh[out0 + h, r : r + 128] = o * (1.0 / o[:, HD : HD + 1])

    for s in range(1, 5):
        heads(2 * (s - 1), 2, qc, kc, vc, 0)
        relay(s)

    @pl.loop(0, 64)
    def _(i):
        ref = tqkv.at[i]

        @pl.when(x < 3)
        def _():
            pltpu.make_async_copy(ref, ref, ts_recv.at[i]).wait()

    def back(i):
        f = lax.rem(i + t, 64)
        return pltpu.make_async_remote_copy(
            src_ref=tout.at[f],
            dst_ref=timed.at[owner],
            send_sem=to_send.at[i],
            recv_sem=to_recv.at[owner],
            device_id=(v4, f),
            device_id_type=MESH,
        )

    @pl.when(x < 3)
    def _():
        a = tqkv[...].reshape(512, 896).astype(f32)
        r = lax.broadcasted_iota(jnp.int32, (512, 512), 0)
        c = lax.broadcasted_iota(jnp.int32, (512, 512), 1)
        other = jnp.where(jnp.bitwise_and(r, 7) == jnp.bitwise_and(c, 7), 0.0, NEG)
        outs = []
        for h in range(TIME_HEADS):
            q = tile(a, HD * h, 0.0)
            k = tile(a, 288 + HD * h, 0.0)
            val = tile(a, 576 + HD * h, 1.0)
            s = lax.dot_general(q, k, (((1,), (1,)), ((), ())), preferred_element_type=f32) + other
            top = jnp.max(s, axis=1, keepdims=True)
            p = jnp.exp2((s - top) * EXP_SCALE).astype(bf)
            o = mm(p, val)
            outs.append(o * (1.0 / o[:, HD : HD + 1]))
        tout[...] = joined(outs).astype(bf).reshape(64, 8, 384)

    for r in range(0, 1024, 256):
        a = bkv[r // 16 : r // 16 + 16].reshape(256, 768).astype(f32)
        fill = a[:, 0:1]
        for h in range(BOX_HEADS):
            kb[h, n + r : n + r + 256] = tile(a, 96 + HD * h, fill)
            vb[h, n + r : n + r + 256] = tile(a, 480 + HD * h, 1.0)

    @pl.when(x < 3)
    def _():
        @pl.loop(0, 64)
        def _(i):
            back(i).start()

    heads(0, BOX_HEADS, qb, kb, vb, CROSS_HEADS)

    total = rows.astype(f32)
    crossed = joined([oh[h] for h in range(CROSS_HEADS)]).astype(bf)
    total += mm(crossed[:, :576], wz_ref[0:576, ZQ:ZW])
    boxed = joined([oh[CROSS_HEADS + h] for h in range(BOX_HEADS)])[:, :288]
    boxed = (boxed * jnp.tanh(gate_ref[...])).astype(bf)
    total += mm(boxed, wz_ref[864:1152, ZQ:ZW])

    @pl.loop(0, 48)
    def _(i):
        ref = timed.at[i]
        pltpu.make_async_copy(ref, ref, to_recv.at[i]).wait()

    both = timed[...].reshape(n, 384)
    total += mm(both[:, :288], wz_ref[576:864, ZQ:ZW])
    out_ref[...] = total.astype(bf)

    @pl.loop(0, 48)
    def _(i):
        time_copy(i).wait_send()

    @pl.when(x < 3)
    def _():
        @pl.loop(0, 64)
        def _(i):
            back(i).wait_send()

    for c in first + sent:
        c.wait_send()


def joined(outs):
    width = -(-len(outs) * HD // 128) * 128
    rows = outs[0].shape[0]
    at = lax.broadcasted_iota(jnp.int32, (rows, 128), 1)
    blank = jnp.zeros((rows, 128), jnp.float32)
    done = []
    for c in range(width // 128):
        piece = blank
        for h, o in enumerate(outs):
            lo = h * HD - c * 128
            if lo >= 128 or lo + HD <= 0:
                continue
            moved = pltpu.roll(o, lo % 128, 1) if lo % 128 else o
            keep = jnp.logical_and(at >= lo, at < lo + HD)
            piece = jnp.where(keep, moved, piece)
        done.append(piece)
    return jnp.concatenate(done, axis=1)


def attend(rows, near, wx, wz, boxes, count, valid, link, gate):
    bf, f32 = jnp.bfloat16, jnp.float32
    vmem = pl.BlockSpec(memory_space=pltpu.VMEM)
    smem = pl.BlockSpec(memory_space=pltpu.SMEM)
    n = TOKENS
    dma = pltpu.SemaphoreType.DMA
    return pl.pallas_call(
        attend_kernel,
        out_shape=jax.ShapeDtypeStruct(rows.shape, bf),
        in_specs=[vmem] * 5 + [smem] * 3 + [vmem],
        out_specs=vmem,
        scratch_shapes=[
            pltpu.VMEM((n, 3 * D), f32),
            pltpu.VMEM((2 * n, 1280), f32),
            pltpu.VMEM((48, 8, 896), bf),
            pltpu.VMEM((64, 8, 896), bf),
            pltpu.VMEM((64, 8, 384), bf),
            pltpu.VMEM((48, 8, 384), bf),
            pltpu.VMEM((16, 768), bf),
            pltpu.VMEM((64, 16, 768), bf),
            pltpu.VMEM((8, n, 128), bf),
            pltpu.VMEM((8, 3 * n, 128), bf),
            pltpu.VMEM((8, 3 * n, 128), bf),
            pltpu.VMEM((4, n, 128), bf),
            pltpu.VMEM((4, n + 1024, 128), bf),
            pltpu.VMEM((4, n + 1024, 128), bf),
            pltpu.VMEM((12, n, 128), f32),
            dma((48,)), dma((64,)), dma((64,)), dma((48,)),
            dma((7,)), dma((8,)), dma((16,)), dma((16,)), dma,
        ],
        compiler_params=pltpu.CompilerParams(
            collective_id=1, has_side_effects=True, vmem_limit_bytes=60 << 20
        ),
        name="attend",
    )(rows, near, wx, wz, boxes, count, valid, link, gate)


def per_device(frames_x, box_embed, box_count, frame_valid, cycle_link, w_qkv, w_out, box_gate):
    rows = frames_x.reshape(TOKENS, D)
    boxes = box_embed.reshape(16, D)
    wx, wz, near = gather(w_qkv, w_out, rows)
    result = attend(
        rows,
        near,
        wx.reshape(4, D, XC),
        wz.reshape(D, ZW),
        boxes,
        box_count,
        frame_valid,
        cycle_link,
        box_gate.reshape(1, BOX_HEADS * HD),
    )
    return result.reshape(frames_x.shape)


def solution(mesh):
    in_specs = (
        P("view", "tm", None, None),
        P("view", "tm", None, None),
        P("view", "tm"),
        P("view", "tm"),
        P("view", None),
        P("tm", None),
        P("tm", None),
        P(),
    )
    out_specs = P("view", "tm", None, None)
    return jax.shard_map(
        per_device, mesh=mesh, in_specs=in_specs, out_specs=out_specs, check_vma=False
    )
```

```python
import jax
import jax.numpy as jnp
from jax import lax
from jax.experimental import pallas as pl
from jax.experimental.pallas import tpu as pltpu
from jax.sharding import PartitionSpec as P

MESH = pl.DeviceIdType.MESH
XC = 768
ZQ = 384
ZW = 1536
QX = 4 * XC
D = 1152
TOKENS = 384
HD = 72
CROSS_HEADS = 8
TIME_HEADS = 4
BOX_HEADS = 4
NEG = -1e30
EXP_SCALE = HD**-0.5 * 1.4426950408889634


def layer_kernel(
    wq, wo, x_ref, box_ref, cnt_ref, val_ref, link_ref, gate_ref, out_ref,
    wx, wz, xn, m, stage,
    qkv, nbr, tsend, tqkv, tout, timed, kvb, bkv, qc, kc, vc, qb, kb, vb, oh,
    ssem, msem, rxs, rzs, nsem, lsem,
    ts_send, ts_recv, to_send, to_recv, ba_send, ba_recv, br_send, br_recv, own_sem,
):
    bf, f32 = jnp.bfloat16, jnp.float32
    n = TOKENS
    v = lax.axis_index("view")
    t = lax.axis_index("tm")
    core = lax.rem(v, 2)
    x = lax.rem(t, 4)
    z = lax.rem(t // 4, 8)
    yh = t // 32
    d = 1 - 2 * core
    up, down = lax.rem(v + 1, 8), lax.rem(v + 7, 8)
    partner = v + 1 - 2 * core
    v4 = lax.rem(v + 4, 8)
    owner = (t // 4) * 3 + x
    base = (t * 3) // 4
    right, left, across = [lax.rem(x + j, 4) for j in (1, 3, 2)]

    def tm(yy, zz, xx):
        return (yy * 8 + zz) * 4 + xx

    def zat(k):
        return lax.rem(z + d * k + 16, 8)

    plane = [tm(yh, z, lax.rem(x + j, 4)) for j in range(1, 4)]
    plane += [tm(1 - yh, z, lax.rem(x + j, 4)) for j in range(4)]
    barrier = pltpu.get_barrier_semaphore()

    @pl.loop(0, 64)
    def _(i):
        pl.semaphore_signal(barrier, inc=1, device_id=(v4, i), device_id_type=MESH)

    for p in plane + [tm(yh, zat(1), x), tm(yh, zat(-1), x)]:
        pl.semaphore_signal(barrier, inc=1, device_id=(v, p), device_id_type=MESH)
    for p in (up, down):
        pl.semaphore_signal(barrier, inc=1, device_id=(p, t), device_id_type=MESH)
    pl.semaphore_wait(barrier, 75)

    sends = []

    def send(src, dst, rsem, to):
        c = pltpu.make_async_remote_copy(
            src_ref=src,
            dst_ref=dst,
            send_sem=ssem.at[len(sends)],
            recv_sem=rsem,
            device_id=to,
            device_id_type=MESH,
        )
        c.start()
        sends.append(c)

    def arrived(ref, sem):
        pltpu.make_async_copy(ref, ref, sem).wait()

    @pl.when(core == yh)
    def _():
        out = []
        for half, view in ((yh, v), (1 - yh, v4)):
            for j in (2, 1, 3, 0):
                xx = lax.rem(x + j, 4)
                cols = pl.ds(pl.multiple_of(xx * XC, 128), XC)
                for k, (src, lo, width) in enumerate(
                    (
                        (wq.at[:, cols], 0, XC),
                        (wq.at[:, pl.ds(QX, ZQ)], XC, ZQ),
                        (wo, XC + ZQ, ZW - ZQ),
                    )
                ):
                    dst = m.at[x, :, pl.ds(lo, width)]
                    if view is v and j == 0:
                        pltpu.make_async_copy(src, dst, msem.at[x, k]).start()
                        continue
                    c = pltpu.make_async_remote_copy(
                        src_ref=src,
                        dst_ref=dst,
                        send_sem=lsem.at[len(out)],
                        recv_sem=msem.at[x, k],
                        device_id=(view, tm(half, z, xx)),
                        device_id_type=MESH,
                    )
                    c.start()
                    out.append(c)
        for c in out:
            c.wait_send()

    row = lax.broadcasted_iota(jnp.int32, (72, 18), 0)
    col = lax.broadcasted_iota(jnp.int32, (72, 18), 1)
    for xx in range(4):
        arrived(m.at[xx, :, pl.ds(0, XC)], msem.at[xx, 0])
        arrived(m.at[xx, :, pl.ds(XC, ZQ)], msem.at[xx, 1])
        arrived(m.at[xx, :, pl.ds(XC + ZQ, ZW - ZQ)], msem.at[xx, 2])
    acc = jnp.zeros((72, XC + ZW), f32)
    for xx in range(4):
        pick = (row == col + 18 * xx).astype(bf)
        acc += jnp.dot(pick, m[xx], preferred_element_type=f32)
    stage[...] = acc.astype(bf)

    mine = core * 8
    b0 = mine + z
    fresh = [
        pltpu.make_async_copy(stage.at[:, pl.ds(0, XC)], wx.at[x, b0], rxs.at[x, b0]),
        pltpu.make_async_copy(stage.at[:, pl.ds(XC, ZW)], wz.at[b0], rzs.at[b0]),
    ]
    for c in fresh:
        c.start()

    def forward(xx, b, to):
        send(wx.at[xx, b], wx.at[xx, b], rxs.at[xx, b], to)

    def spread(b, srcx, srcz, nxt):
        for k in nxt:
            send(srcx, wx.at[x, b], rxs.at[x, b], (v, tm(yh, k, x)))
            send(srcz, wz.at[b], rzs.at[b], (v, tm(yh, k, x)))
        for xx in (right, left):
            send(srcx, wx.at[x, b], rxs.at[x, b], (v, tm(yh, z, xx)))
        send(srcx, wx.at[x, b], rxs.at[x, b], (partner, t))
        send(srcz, wz.at[b], rzs.at[b], (partner, t))

    def relay_x(b, sign):
        arrived(wx.at[left, b], rxs.at[left, b])
        if sign > 0:
            forward(left, b, (v, tm(yh, z, right)))
        forward(left, b, (partner, t))
        arrived(wx.at[right, b], rxs.at[right, b])
        if sign < 0:
            forward(right, b, (v, tm(yh, z, left)))
        forward(right, b, (partner, t))

    def last_x(b):
        arrived(wx.at[across, b], rxs.at[across, b])
        forward(across, b, (partner, t))

    spread(b0, stage.at[:, pl.ds(0, XC)], stage.at[:, pl.ds(XC, ZW)], (zat(1), zat(-1)))
    send(x_ref, xn.at[0], nsem.at[0], (up, t))
    send(x_ref, xn.at[1], nsem.at[1], (down, t))
    todo, late = [(b0, -1)], []
    for s in range(1, 5):
        for sign in (1, -1):
            if sign < 0 and s == 4:
                continue
            b = mine + zat(-s * sign)
            arrived(wx.at[x, b], rxs.at[x, b])
            arrived(wz.at[b], rzs.at[b])
            last = s == 4 or (sign < 0 and s == 3)
            spread(b, wx.at[x, b], wz.at[b], () if last else (zat(sign),))
            todo.append((b, sign))
            b, sign = todo.pop(0)
            relay_x(b, sign)
            late.append(b)
            if len(late) > 2:
                last_x(late.pop(0))
    for b, sign in todo:
        relay_x(b, sign)
        late.append(b)
    for b in late:
        last_x(b)
    for c in fresh:
        c.wait()
    other = 8 - mine
    for k in range(8):
        b = other + k
        arrived(wz.at[b], rzs.at[b])
        for xx in range(4):
            arrived(wx.at[xx, b], rxs.at[xx, b])

    def mm(a, b):
        return jnp.dot(a, b, preferred_element_type=f32)

    def chunk(i, lo, hi):
        return wx[i, :, :, lo:hi].reshape(D, hi - lo)

    def tail(lo, hi):
        return wz[:, :, lo:hi].reshape(D, hi - lo)

    boxes = box_ref[...]
    bk = jnp.concatenate([mm(boxes, chunk(2, 384, 768)), mm(boxes, tail(0, 384))], axis=1)
    slot = lax.broadcasted_iota(jnp.int32, (16, 768), 0)
    blane = lax.broadcasted_iota(jnp.int32, (16, 768), 1)
    live = jnp.logical_and(slot < cnt_ref[0, 0], val_ref[0, 0] == 1)
    bv = jnp.where(blane < 288, pltpu.roll(bk, 768 - 96, 1), pltpu.roll(bk, 768 - 192, 1))
    bv = jnp.where(blane == 576, jnp.where(live, 0.0, NEG), bv)
    kvb[...] = bv[:, :640].astype(bf)

    rows = x_ref[...]
    qkv[:, 0:XC] = mm(rows, chunk(0, 0, XC))

    own = pltpu.make_async_copy(kvb, bkv.at[t], own_sem)
    own.start()
    first = []
    for k, p in enumerate(plane):
        c = pltpu.make_async_remote_copy(
            src_ref=kvb,
            dst_ref=bkv.at[t],
            send_sem=ba_send.at[k],
            recv_sem=ba_recv.at[yh * 4 + x],
            device_id=(v, p),
            device_id_type=MESH,
        )
        c.start()
        first.append(c)

    for i in range(1, 4):
        qkv[:, i * XC : (i + 1) * XC] = mm(rows, chunk(i, 0, XC))
    qkv[:, QX : QX + ZQ] = mm(rows, tail(0, ZQ))

    tq = [qkv[:, c * 128 : c * 128 + 896] for c in (4, 13)]
    tq.append(jnp.concatenate([qkv[:, 2816:3456], qkv[:, 0:256]], axis=1))
    lane = lax.broadcasted_iota(jnp.int32, (n, 896), 1)
    packed = pltpu.roll(tq[0], 896 - 64, 1)
    packed = jnp.where(lane < 288, packed, pltpu.roll(tq[1], 288 - 64, 1))
    packed = jnp.where(lane < 576, packed, pltpu.roll(tq[2], 576 - 64, 1))
    tsend[...] = packed.astype(bf).reshape(48, 8, 896)

    def time_copy(i):
        o = lax.rem(i + base, 48)
        return pltpu.make_async_remote_copy(
            src_ref=tsend.at[o],
            dst_ref=tqkv.at[t],
            send_sem=ts_send.at[i],
            recv_sem=ts_recv.at[t],
            device_id=(v4, (o // 3) * 4 + lax.rem(o, 3)),
            device_id_type=MESH,
        )

    def send_time(lo, hi):
        @pl.loop(lo, hi)
        def _(i):
            time_copy(i).start()

    own.wait()
    for yy in range(2):
        for j in range(4):
            if yy or j:
                half, xx = lax.rem(yh + yy, 2), lax.rem(x + j, 4)
                arrived(bkv.at[tm(half, z, xx)], ba_recv.at[half * 4 + xx])

    def group(yy, zz):
        return bkv.at[pl.ds(tm(yy, zz, 0), 4)]

    def ring(yy, zz, to, k):
        return pltpu.make_async_remote_copy(
            src_ref=group(yy, zz),
            dst_ref=group(yy, zz),
            send_sem=br_send.at[k],
            recv_sem=br_recv.at[yy * 8 + zz],
            device_id=(v, tm(yh, to, x)),
            device_id_type=MESH,
        )

    sent = []

    def start(c):
        c.start()
        sent.append(c)

    for yy in range(2):
        for sign in (1, -1):
            start(ring(yy, z, zat(sign), len(sent)))

    def relay(s):
        for sign in (1, -1):
            if sign < 0 and s == 4:
                continue
            zz = zat(-s * sign)
            for yy in range(2):
                arrived(group(yy, zz), br_recv.at[yy * 8 + zz])
                if s < (4 if sign > 0 else 3):
                    start(ring(yy, zz, zat(sign), len(sent)))

    send_time(0, 24)

    arrived(xn.at[0], nsem.at[0])
    arrived(xn.at[1], nsem.at[1])
    near = xn[...].reshape(2 * n, D)
    nbr[:, 0:384] = mm(near, chunk(1, 384, 768))
    nbr[:, 384:640] = mm(near, chunk(2, 0, 256))
    nbr[:, 640:1280] = mm(near, chunk(3, 0, 640))

    def tile(a, off, fill):
        piece = pltpu.roll(a, (a.shape[1] - off) % a.shape[1], 1)[:, :128] if off else a[:, :128]
        at = lax.broadcasted_iota(jnp.int32, piece.shape, 1)
        return jnp.where(at < HD, piece, jnp.where(at == HD, fill, 0.0)).astype(bf)

    def head(ref, r0, r1, c, fill):
        lo = c // 128 * 128
        a = ref[r0:r1, lo : min(lo + 256, ref.shape[1])]
        return tile(a, c - lo, fill)

    gone = [jnp.where(link_ref[0, i] > 0, 0.0, NEG) for i in range(2)]
    for h in range(CROSS_HEADS):
        qc[h] = head(qkv, 0, n, HD * h, 1.0)
        for s, (ref, r0, ck, cv, fill) in enumerate(
            (
                (nbr, 0, 0, 640, gone[0]),
                (qkv, 0, D, 2 * D, 0.0),
                (nbr, n, 0, 640, gone[1]),
            )
        ):
            kc[h, s * n : (s + 1) * n] = head(ref, r0, r0 + n, ck + HD * h, fill)
            vc[h, s * n : (s + 1) * n] = head(ref, r0, r0 + n, cv + HD * h, 1.0)
    at0 = (CROSS_HEADS + TIME_HEADS) * HD
    for h in range(BOX_HEADS):
        qb[h] = head(qkv, 0, n, at0 + HD * h, 1.0)
        kb[h, 0:n] = head(qkv, 0, n, D + at0 + HD * h, 0.0)
        vb[h, 0:n] = head(qkv, 0, n, 2 * D + at0 + HD * h, 1.0)

    def softmax_dot(q, k, val):
        s = lax.dot_general(q, k, (((1,), (1,)), ((), ())), preferred_element_type=f32)
        top = jnp.max(s, axis=1, keepdims=True)
        p = jnp.exp2((s - top) * EXP_SCALE).astype(bf)
        return mm(p, val)

    def heads(first_head, count, q_ref, k_ref, v_ref, out0):
        @pl.loop(first_head, first_head + count)
        def _(h):
            for r in range(0, n, 128):
                o = softmax_dot(q_ref[h, r : r + 128], k_ref[h], v_ref[h])
                oh[out0 + h, r : r + 128] = o * (1.0 / o[:, HD : HD + 1])

    for s in range(1, 5):
        relay(s)
        if s == 1:
            send_time(24, 48)
        heads(2 * (s - 1), 2, qc, kc, vc, 0)

    @pl.loop(0, 64)
    def _(i):
        ref = tqkv.at[i]

        @pl.when(x < 3)
        def _():
            pltpu.make_async_copy(ref, ref, ts_recv.at[i]).wait()

    def back(i):
        f = lax.rem(i + t, 64)
        return pltpu.make_async_remote_copy(
            src_ref=tout.at[f],
            dst_ref=timed.at[owner],
            send_sem=to_send.at[i],
            recv_sem=to_recv.at[owner],
            device_id=(v4, f),
            device_id_type=MESH,
        )

    @pl.when(x < 3)
    def _():
        a = tqkv[...].reshape(512, 896).astype(f32)
        r = lax.broadcasted_iota(jnp.int32, (512, 512), 0)
        c = lax.broadcasted_iota(jnp.int32, (512, 512), 1)
        other = jnp.where(jnp.bitwise_and(r, 7) == jnp.bitwise_and(c, 7), 0.0, NEG)
        outs = []
        for h in range(TIME_HEADS):
            q = tile(a, HD * h, 0.0)
            k = tile(a, 288 + HD * h, 0.0)
            val = tile(a, 576 + HD * h, 1.0)
            s = lax.dot_general(q, k, (((1,), (1,)), ((), ())), preferred_element_type=f32) + other
            top = jnp.max(s, axis=1, keepdims=True)
            p = jnp.exp2((s - top) * EXP_SCALE).astype(bf)
            o = mm(p, val)
            outs.append(o * (1.0 / o[:, HD : HD + 1]))
        tout[...] = joined(outs).astype(bf).reshape(64, 8, 384)

    for r in range(0, 1024, 256):
        a = bkv[r // 16 : r // 16 + 16].reshape(256, 640).astype(f32)
        fill = a[:, 576:577]
        for h in range(BOX_HEADS):
            kb[h, n + r : n + r + 256] = tile(a, HD * h, fill)
            vb[h, n + r : n + r + 256] = tile(a, 288 + HD * h, 1.0)

    @pl.when(x < 3)
    def _():
        @pl.loop(0, 64)
        def _(i):
            back(i).start()

    heads(0, BOX_HEADS, qb, kb, vb, CROSS_HEADS)

    total = rows.astype(f32)
    crossed = joined([oh[h] for h in range(CROSS_HEADS)]).astype(bf)
    total += mm(crossed[:, :576], wz[0:8, :, ZQ:ZW].reshape(576, D))
    boxed = joined([oh[CROSS_HEADS + h] for h in range(BOX_HEADS)])[:, :288]
    boxed = (boxed * jnp.tanh(gate_ref[...].reshape(1, BOX_HEADS * HD))).astype(bf)
    total += mm(boxed, wz[12:16, :, ZQ:ZW].reshape(288, D))

    @pl.loop(0, 48)
    def _(i):
        ref = timed.at[i]
        pltpu.make_async_copy(ref, ref, to_recv.at[i]).wait()

    both = timed[...].reshape(n, 384)
    total += mm(both[:, :288], wz[8:12, :, ZQ:ZW].reshape(288, D))
    out_ref[...] = total.astype(bf)

    @pl.loop(0, 48)
    def _(i):
        time_copy(i).wait_send()

    @pl.when(x < 3)
    def _():
        @pl.loop(0, 64)
        def _(i):
            back(i).wait_send()

    for c in sends + first + sent:
        c.wait_send()


def joined(outs):
    width = -(-len(outs) * HD // 128) * 128
    rows = outs[0].shape[0]
    at = lax.broadcasted_iota(jnp.int32, (rows, 128), 1)
    blank = jnp.zeros((rows, 128), jnp.float32)
    done = []
    for c in range(width // 128):
        piece = blank
        for h, o in enumerate(outs):
            lo = h * HD - c * 128
            if lo >= 128 or lo + HD <= 0:
                continue
            moved = pltpu.roll(o, lo % 128, 1) if lo % 128 else o
            keep = jnp.logical_and(at >= lo, at < lo + HD)
            piece = jnp.where(keep, moved, piece)
        done.append(piece)
    return jnp.concatenate(done, axis=1)


def layer(w_qkv, w_out, rows, boxes, count, valid, link, gate):
    bf, f32 = jnp.bfloat16, jnp.float32
    hbm = pl.BlockSpec(memory_space=pl.ANY)
    vmem = pl.BlockSpec(memory_space=pltpu.VMEM)
    smem = pl.BlockSpec(memory_space=pltpu.SMEM)
    n = TOKENS
    dma = pltpu.SemaphoreType.DMA
    return pl.pallas_call(
        layer_kernel,
        out_shape=jax.ShapeDtypeStruct(rows.shape, bf),
        in_specs=[hbm] * 2 + [vmem] * 2 + [smem] * 3 + [vmem],
        out_specs=vmem,
        scratch_shapes=[
            pltpu.VMEM((4, 16, 72, XC), bf),
            pltpu.VMEM((16, 72, ZW), bf),
            pltpu.VMEM((2, n, D), bf),
            pltpu.VMEM((4, 18, XC + ZW), bf),
            pltpu.VMEM((72, XC + ZW), bf),
            pltpu.VMEM((n, 3 * D), f32),
            pltpu.VMEM((2 * n, 1280), f32),
            pltpu.VMEM((48, 8, 896), bf),
            pltpu.VMEM((64, 8, 896), bf),
            pltpu.VMEM((64, 8, 384), bf),
            pltpu.VMEM((48, 8, 384), bf),
            pltpu.VMEM((16, 640), bf),
            pltpu.VMEM((64, 16, 640), bf),
            pltpu.VMEM((8, n, 128), bf),
            pltpu.VMEM((8, 3 * n, 128), bf),
            pltpu.VMEM((8, 3 * n, 128), bf),
            pltpu.VMEM((4, n, 128), bf),
            pltpu.VMEM((4, n + 1024, 128), bf),
            pltpu.VMEM((4, n + 1024, 128), bf),
            pltpu.VMEM((12, n, 128), f32),
            dma((90,)), dma((4, 3)), dma((4, 16)), dma((16,)), dma((2,)), dma((21,)),
            dma((48,)), dma((64,)), dma((64,)), dma((48,)),
            dma((7,)), dma((8,)), dma((16,)), dma((16,)), dma,
        ],
        compiler_params=pltpu.CompilerParams(
            collective_id=0, has_side_effects=True, vmem_limit_bytes=60 << 20
        ),
        name="layer",
    )(w_qkv, w_out, rows, boxes, count, valid, link, gate)


def per_device(frames_x, box_embed, box_count, frame_valid, cycle_link, w_qkv, w_out, box_gate):
    result = layer(
        w_qkv,
        w_out,
        frames_x.reshape(TOKENS, D),
        box_embed.reshape(16, D),
        box_count,
        frame_valid,
        cycle_link,
        box_gate,
    )
    return result.reshape(frames_x.shape)


def solution(mesh):
    in_specs = (
        P("view", "tm", None, None),
        P("view", "tm", None, None),
        P("view", "tm"),
        P("view", "tm"),
        P("view", None),
        P("tm", None),
        P("tm", None),
        P(),
    )
    out_specs = P("view", "tm", None, None)
    return jax.shard_map(
        per_device, mesh=mesh, in_specs=in_specs, out_specs=out_specs, check_vma=False
    )
```

```python
import jax
import jax.numpy as jnp
from jax import lax
from jax.experimental import pallas as pl
from jax.experimental.pallas import tpu as pltpu
from jax.sharding import PartitionSpec as P

MESH = pl.DeviceIdType.MESH
XC = 768
ZQ = 384
ZW = 1536
QX = 4 * XC
D = 1152
TOKENS = 384
HD = 72
CROSS_HEADS = 8
TIME_HEADS = 4
BOX_HEADS = 4
NEG = -1e30
EXP_SCALE = HD**-0.5 * 1.4426950408889634


def layer_kernel(
    wq, wo, x_ref, box_ref, cnt_ref, val_ref, link_ref, gate_ref, out_ref,
    wx, wz, xn, m, stage,
    qkv, nbr, tsend, tqkv, tout, timed, kvb, bkv, qc, kc, vc, qb, kb, vb, oh,
    ssem, msem, rxs, rzs, nsem, lsem,
    ts_send, ts_recv, to_send, to_recv, br_send, br_recv, own_sem,
):
    bf, f32 = jnp.bfloat16, jnp.float32
    n = TOKENS
    v = lax.axis_index("view")
    t = lax.axis_index("tm")
    core = lax.rem(v, 2)
    x = lax.rem(t, 4)
    z = lax.rem(t // 4, 8)
    yh = t // 32
    d = 1 - 2 * core
    up, down = lax.rem(v + 1, 8), lax.rem(v + 7, 8)
    partner = v + 1 - 2 * core
    v4 = lax.rem(v + 4, 8)
    owner = (t // 4) * 3 + x
    base = (t * 3) // 4
    right, left, across = [lax.rem(x + j, 4) for j in (1, 3, 2)]

    def tm(yy, zz, xx):
        return (yy * 8 + zz) * 4 + xx

    def zat(k):
        return lax.rem(z + d * k + 16, 8)

    plane = [tm(yh, z, lax.rem(x + j, 4)) for j in range(1, 4)] + [tm(1 - yh, z, x)]
    barrier = pltpu.get_barrier_semaphore()

    @pl.loop(0, 64)
    def _(i):
        pl.semaphore_signal(barrier, inc=1, device_id=(v4, i), device_id_type=MESH)

    for p in plane + [tm(yh, zat(1), x), tm(yh, zat(-1), x)]:
        pl.semaphore_signal(barrier, inc=1, device_id=(v, p), device_id_type=MESH)
    for p in (up, down):
        pl.semaphore_signal(barrier, inc=1, device_id=(p, t), device_id_type=MESH)
    pl.semaphore_wait(barrier, 72)

    sends = []

    def send(src, dst, rsem, to):
        c = pltpu.make_async_remote_copy(
            src_ref=src,
            dst_ref=dst,
            send_sem=ssem.at[len(sends)],
            recv_sem=rsem,
            device_id=to,
            device_id_type=MESH,
        )
        c.start()
        sends.append(c)

    def arrived(ref, sem):
        pltpu.make_async_copy(ref, ref, sem).wait()

    @pl.when(core == yh)
    def _():
        out = []
        for half, view in ((yh, v), (1 - yh, v4)):
            for j in (2, 1, 3, 0):
                xx = lax.rem(x + j, 4)
                cols = pl.ds(pl.multiple_of(xx * XC, 128), XC)
                for k, (src, lo, width) in enumerate(
                    (
                        (wq.at[:, cols], 0, XC),
                        (wq.at[:, pl.ds(QX, ZQ)], XC, ZQ),
                        (wo, XC + ZQ, ZW - ZQ),
                    )
                ):
                    dst = m.at[x, :, pl.ds(lo, width)]
                    if view is v and j == 0:
                        pltpu.make_async_copy(src, dst, msem.at[x, k]).start()
                        continue
                    c = pltpu.make_async_remote_copy(
                        src_ref=src,
                        dst_ref=dst,
                        send_sem=lsem.at[len(out)],
                        recv_sem=msem.at[x, k],
                        device_id=(view, tm(half, z, xx)),
                        device_id_type=MESH,
                    )
                    c.start()
                    out.append(c)
        for c in out:
            c.wait_send()

    row = lax.broadcasted_iota(jnp.int32, (72, 18), 0)
    col = lax.broadcasted_iota(jnp.int32, (72, 18), 1)
    for xx in range(4):
        arrived(m.at[xx, :, pl.ds(0, XC)], msem.at[xx, 0])
        arrived(m.at[xx, :, pl.ds(XC, ZQ)], msem.at[xx, 1])
        arrived(m.at[xx, :, pl.ds(XC + ZQ, ZW - ZQ)], msem.at[xx, 2])
    acc = jnp.zeros((72, XC + ZW), f32)
    for xx in range(4):
        pick = (row == col + 18 * xx).astype(bf)
        acc += jnp.dot(pick, m[xx], preferred_element_type=f32)
    stage[...] = acc.astype(bf)

    mine = core * 8
    b0 = mine + z
    fresh = [
        pltpu.make_async_copy(stage.at[:, pl.ds(0, XC)], wx.at[x, b0], rxs.at[x, b0]),
        pltpu.make_async_copy(stage.at[:, pl.ds(XC, ZW)], wz.at[b0], rzs.at[b0]),
    ]
    for c in fresh:
        c.start()

    def forward(xx, b, to):
        send(wx.at[xx, b], wx.at[xx, b], rxs.at[xx, b], to)

    def spread_x(b, src, nxt):
        for k in nxt:
            send(src, wx.at[x, b], rxs.at[x, b], (v, tm(yh, k, x)))
        for xx in (right, left):
            send(src, wx.at[x, b], rxs.at[x, b], (v, tm(yh, z, xx)))
        send(src, wx.at[x, b], rxs.at[x, b], (partner, t))

    def spread_z(b, src, nxt):
        for k in nxt:
            send(src, wz.at[b], rzs.at[b], (v, tm(yh, k, x)))
        send(src, wz.at[b], rzs.at[b], (partner, t))

    def relay_x(b, sign):
        arrived(wx.at[left, b], rxs.at[left, b])
        if sign > 0:
            forward(left, b, (v, tm(yh, z, right)))
        forward(left, b, (partner, t))
        arrived(wx.at[right, b], rxs.at[right, b])
        if sign < 0:
            forward(right, b, (v, tm(yh, z, left)))
        forward(right, b, (partner, t))

    def last_x(b):
        arrived(wx.at[across, b], rxs.at[across, b])
        forward(across, b, (partner, t))

    spread_x(b0, stage.at[:, pl.ds(0, XC)], (zat(1), zat(-1)))
    spread_z(b0, stage.at[:, pl.ds(XC, ZW)], (zat(1), zat(-1)))
    send(x_ref, xn.at[0], nsem.at[0], (up, t))
    send(x_ref, xn.at[1], nsem.at[1], (down, t))
    todo, late = [(b0, -1)], []
    for s in range(1, 5):
        signs = (1, -1) if s < 4 else (1,)
        for sign in signs:
            b = mine + zat(-s * sign)
            arrived(wx.at[x, b], rxs.at[x, b])
            spread_x(b, wx.at[x, b], (zat(sign),) if s < (4 if sign > 0 else 3) else ())
        for sign in signs:
            b = mine + zat(-s * sign)
            arrived(wz.at[b], rzs.at[b])
            spread_z(b, wz.at[b], (zat(sign),) if s < (4 if sign > 0 else 3) else ())
            todo.append((b, sign))
            b, sign = todo.pop(0)
            relay_x(b, sign)
            late.append(b)
            if len(late) > 2:
                last_x(late.pop(0))
    for b, sign in todo:
        relay_x(b, sign)
        late.append(b)
    for b in late:
        last_x(b)
    for c in fresh:
        c.wait()
    other = 8 - mine
    for k in range(8):
        b = other + k
        arrived(wz.at[b], rzs.at[b])
        for xx in range(4):
            arrived(wx.at[xx, b], rxs.at[xx, b])

    def mm(a, b):
        return jnp.dot(a, b, preferred_element_type=f32)

    def chunk(i, lo, hi):
        return wx[i, :, :, lo:hi].reshape(D, hi - lo)

    def tail(lo, hi):
        return wz[:, :, lo:hi].reshape(D, hi - lo)

    boxes = box_ref[...]
    bk = jnp.concatenate([mm(boxes, chunk(2, 384, 768)), mm(boxes, tail(0, 384))], axis=1)
    slot = lax.broadcasted_iota(jnp.int32, (16, 768), 0)
    blane = lax.broadcasted_iota(jnp.int32, (16, 768), 1)
    live = jnp.logical_and(slot < cnt_ref[0, 0], val_ref[0, 0] == 1)
    bv = jnp.where(blane < 288, pltpu.roll(bk, 768 - 96, 1), pltpu.roll(bk, 768 - 192, 1))
    bv = jnp.where(blane == 576, jnp.where(live, 0.0, NEG), bv)
    kvb[...] = bv[:, :640].astype(bf)

    rows = x_ref[...]
    spots = (
        (512, chunk(0, 512, 768)),
        (768, chunk(1, 0, 128)),
        (1664, chunk(2, 128, 512)),
        (2816, chunk(3, 512, 768)),
        (3072, tail(0, 128)),
    )
    for lo, w in spots:
        qkv[:, lo : lo + w.shape[1]] = mm(rows, w)
    lane = lax.broadcasted_iota(jnp.int32, (n, 896), 1)
    blank = jnp.zeros((n, 512), f32)
    parts = [
        pltpu.roll(jnp.concatenate([qkv[:, lo : lo + 384], blank], axis=1), shift, 1)
        for lo, shift in ((512, 896 - 64), (1664, 288 - 64), (2816, 576 - 64))
    ]
    packed = jnp.where(lane < 288, parts[0], jnp.where(lane < 576, parts[1], parts[2]))
    tsend[...] = packed.astype(bf).reshape(48, 8, 896)

    def time_copy(i):
        o = lax.rem(i + base, 48)
        return pltpu.make_async_remote_copy(
            src_ref=tsend.at[o],
            dst_ref=tqkv.at[t],
            send_sem=ts_send.at[i],
            recv_sem=ts_recv.at[t],
            device_id=(v4, (o // 3) * 4 + lax.rem(o, 3)),
            device_id_type=MESH,
        )

    def send_time(lo, hi):
        @pl.loop(lo, hi)
        def _(i):
            time_copy(i).start()

    sent = []

    def pass_on(slot, to, src=None):
        c = pltpu.make_async_remote_copy(
            src_ref=bkv.at[slot] if src is None else src,
            dst_ref=bkv.at[slot],
            send_sem=br_send.at[len(sent)],
            recv_sem=br_recv.at[slot],
            device_id=(v, to),
            device_id_type=MESH,
        )
        c.start()
        sent.append(c)

    def landed(slot):
        arrived(bkv.at[slot], br_recv.at[slot])

    own = pltpu.make_async_copy(kvb, bkv.at[t], own_sem)
    own.start()
    pass_on(t, tm(1 - yh, z, x), kvb)
    for to in (tm(yh, zat(1), x), tm(yh, zat(-1), x), tm(yh, z, right), tm(yh, z, left)):
        pass_on(t, to, kvb)
    send_time(0, 16)

    spots = (
        (0, chunk(0, 0, 512)),
        (896, chunk(1, 128, 768)),
        (1536, chunk(2, 0, 128)),
        (2048, chunk(2, 512, 768)),
        (2304, chunk(3, 0, 512)),
        (3200, tail(128, 384)),
    )
    for lo, w in spots:
        qkv[:, lo : lo + w.shape[1]] = mm(rows, w)

    own.wait()
    landed(tm(1 - yh, z, x))
    for to in (tm(yh, zat(1), x), tm(yh, zat(-1), x), tm(yh, z, right), tm(yh, z, left)):
        pass_on(tm(1 - yh, z, x), to)

    boxes_x, boxes_late = [(z, -1)], []

    def relay(s):
        for sign in (1, -1) if s < 4 else (1,):
            zz = zat(-s * sign)
            for half in (yh, 1 - yh):
                slot = tm(half, zz, x)
                landed(slot)
                if s < (4 if sign > 0 else 3):
                    pass_on(slot, tm(yh, zat(sign), x))
                pass_on(slot, tm(yh, z, right))
                pass_on(slot, tm(yh, z, left))
            boxes_x.append((zz, sign))

    def relay_boxes(keep):
        while len(boxes_x) > keep:
            zz, sign = boxes_x.pop(0)
            for half in (yh, 1 - yh):
                landed(tm(half, zz, left))
                if sign > 0:
                    pass_on(tm(half, zz, left), tm(yh, z, right))
                landed(tm(half, zz, right))
                if sign < 0:
                    pass_on(tm(half, zz, right), tm(yh, z, left))
            boxes_late.append(zz)

    send_time(16, 32)

    arrived(xn.at[0], nsem.at[0])
    arrived(xn.at[1], nsem.at[1])
    near = xn[...].reshape(2 * n, D)
    nbr[:, 0:384] = mm(near, chunk(1, 384, 768))
    nbr[:, 384:640] = mm(near, chunk(2, 0, 256))
    nbr[:, 640:1280] = mm(near, chunk(3, 0, 640))

    relay(1)
    relay_boxes(2)
    send_time(32, 48)

    def tile(a, off, fill):
        piece = pltpu.roll(a, (a.shape[1] - off) % a.shape[1], 1)[:, :128] if off else a[:, :128]
        at = lax.broadcasted_iota(jnp.int32, piece.shape, 1)
        return jnp.where(at < HD, piece, jnp.where(at == HD, fill, 0.0)).astype(bf)

    def head(ref, r0, r1, c, fill):
        lo = c // 128 * 128
        a = ref[r0:r1, lo : min(lo + 256, ref.shape[1])]
        return tile(a, c - lo, fill)

    gone = [jnp.where(link_ref[0, i] > 0, 0.0, NEG) for i in range(2)]
    for h in range(CROSS_HEADS):
        qc[h] = head(qkv, 0, n, HD * h, 1.0)
        for s, (ref, r0, ck, cv, fill) in enumerate(
            (
                (nbr, 0, 0, 640, gone[0]),
                (qkv, 0, D, 2 * D, 0.0),
                (nbr, n, 0, 640, gone[1]),
            )
        ):
            kc[h, s * n : (s + 1) * n] = head(ref, r0, r0 + n, ck + HD * h, fill)
            vc[h, s * n : (s + 1) * n] = head(ref, r0, r0 + n, cv + HD * h, 1.0)
    at0 = (CROSS_HEADS + TIME_HEADS) * HD
    for h in range(BOX_HEADS):
        qb[h] = head(qkv, 0, n, at0 + HD * h, 1.0)
        kb[h, 0:n] = head(qkv, 0, n, D + at0 + HD * h, 0.0)
        vb[h, 0:n] = head(qkv, 0, n, 2 * D + at0 + HD * h, 1.0)

    def softmax_dot(q, k, val):
        s = lax.dot_general(q, k, (((1,), (1,)), ((), ())), preferred_element_type=f32)
        top = jnp.max(s, axis=1, keepdims=True)
        p = jnp.exp2((s - top) * EXP_SCALE).astype(bf)
        return mm(p, val)

    def heads(first_head, count, q_ref, k_ref, v_ref, out0):
        @pl.loop(first_head, first_head + count)
        def _(h):
            for r in range(0, n, 128):
                o = softmax_dot(q_ref[h, r : r + 128], k_ref[h], v_ref[h])
                oh[out0 + h, r : r + 128] = o * (1.0 / o[:, HD : HD + 1])

    for s in range(1, 5):
        if s > 1:
            relay(s)
            relay_boxes(2)
        heads(2 * (s - 1), 2, qc, kc, vc, 0)
    relay_boxes(0)

    @pl.loop(0, 64)
    def _(i):
        ref = tqkv.at[i]

        @pl.when(x < 3)
        def _():
            pltpu.make_async_copy(ref, ref, ts_recv.at[i]).wait()

    def back(i):
        f = lax.rem(i + t, 64)
        return pltpu.make_async_remote_copy(
            src_ref=tout.at[f],
            dst_ref=timed.at[owner],
            send_sem=to_send.at[i],
            recv_sem=to_recv.at[owner],
            device_id=(v4, f),
            device_id_type=MESH,
        )

    @pl.when(x < 3)
    def _():
        a = tqkv[...].reshape(512, 896).astype(f32)
        r = lax.broadcasted_iota(jnp.int32, (512, 512), 0)
        c = lax.broadcasted_iota(jnp.int32, (512, 512), 1)
        other = jnp.where(jnp.bitwise_and(r, 7) == jnp.bitwise_and(c, 7), 0.0, NEG)
        outs = []
        for h in range(TIME_HEADS):
            q = tile(a, HD * h, 0.0)
            k = tile(a, 288 + HD * h, 0.0)
            val = tile(a, 576 + HD * h, 1.0)
            s = lax.dot_general(q, k, (((1,), (1,)), ((), ())), preferred_element_type=f32) + other
            top = jnp.max(s, axis=1, keepdims=True)
            p = jnp.exp2((s - top) * EXP_SCALE).astype(bf)
            o = mm(p, val)
            outs.append(o * (1.0 / o[:, HD : HD + 1]))
        tout[...] = joined(outs).astype(bf).reshape(64, 8, 384)

    for zz in boxes_late:
        for half in (yh, 1 - yh):
            landed(tm(half, zz, across))
    for r in range(0, 1024, 256):
        a = bkv[r // 16 : r // 16 + 16].reshape(256, 640).astype(f32)
        fill = a[:, 576:577]
        for h in range(BOX_HEADS):
            kb[h, n + r : n + r + 256] = tile(a, HD * h, fill)
            vb[h, n + r : n + r + 256] = tile(a, 288 + HD * h, 1.0)

    @pl.when(x < 3)
    def _():
        @pl.loop(0, 64)
        def _(i):
            back(i).start()

    heads(0, BOX_HEADS, qb, kb, vb, CROSS_HEADS)

    total = rows.astype(f32)
    crossed = joined([oh[h] for h in range(CROSS_HEADS)]).astype(bf)
    total += mm(crossed[:, :576], wz[0:8, :, ZQ:ZW].reshape(576, D))
    boxed = joined([oh[CROSS_HEADS + h] for h in range(BOX_HEADS)])[:, :288]
    boxed = (boxed * jnp.tanh(gate_ref[...].reshape(1, BOX_HEADS * HD))).astype(bf)
    total += mm(boxed, wz[12:16, :, ZQ:ZW].reshape(288, D))

    @pl.loop(0, 48)
    def _(i):
        ref = timed.at[i]
        pltpu.make_async_copy(ref, ref, to_recv.at[i]).wait()

    both = timed[...].reshape(n, 384)
    total += mm(both[:, :288], wz[8:12, :, ZQ:ZW].reshape(288, D))
    out_ref[...] = total.astype(bf)

    @pl.loop(0, 48)
    def _(i):
        time_copy(i).wait_send()

    @pl.when(x < 3)
    def _():
        @pl.loop(0, 64)
        def _(i):
            back(i).wait_send()

    for c in sends + sent:
        c.wait_send()


def joined(outs):
    width = -(-len(outs) * HD // 128) * 128
    rows = outs[0].shape[0]
    at = lax.broadcasted_iota(jnp.int32, (rows, 128), 1)
    blank = jnp.zeros((rows, 128), jnp.float32)
    done = []
    for c in range(width // 128):
        piece = blank
        for h, o in enumerate(outs):
            lo = h * HD - c * 128
            if lo >= 128 or lo + HD <= 0:
                continue
            moved = pltpu.roll(o, lo % 128, 1) if lo % 128 else o
            keep = jnp.logical_and(at >= lo, at < lo + HD)
            piece = jnp.where(keep, moved, piece)
        done.append(piece)
    return jnp.concatenate(done, axis=1)


def layer(w_qkv, w_out, rows, boxes, count, valid, link, gate):
    bf, f32 = jnp.bfloat16, jnp.float32
    hbm = pl.BlockSpec(memory_space=pl.ANY)
    vmem = pl.BlockSpec(memory_space=pltpu.VMEM)
    smem = pl.BlockSpec(memory_space=pltpu.SMEM)
    n = TOKENS
    dma = pltpu.SemaphoreType.DMA
    return pl.pallas_call(
        layer_kernel,
        out_shape=jax.ShapeDtypeStruct(rows.shape, bf),
        in_specs=[hbm] * 2 + [vmem] * 2 + [smem] * 3 + [vmem],
        out_specs=vmem,
        scratch_shapes=[
            pltpu.VMEM((4, 16, 72, XC), bf),
            pltpu.VMEM((16, 72, ZW), bf),
            pltpu.VMEM((2, n, D), bf),
            pltpu.VMEM((4, 18, XC + ZW), bf),
            pltpu.VMEM((72, XC + ZW), bf),
            pltpu.VMEM((n, 3 * D), f32),
            pltpu.VMEM((2 * n, 1280), f32),
            pltpu.VMEM((48, 8, 896), bf),
            pltpu.VMEM((64, 8, 896), bf),
            pltpu.VMEM((64, 8, 384), bf),
            pltpu.VMEM((48, 8, 384), bf),
            pltpu.VMEM((16, 640), bf),
            pltpu.VMEM((64, 16, 640), bf),
            pltpu.VMEM((8, n, 128), bf),
            pltpu.VMEM((8, 3 * n, 128), bf),
            pltpu.VMEM((8, 3 * n, 128), bf),
            pltpu.VMEM((4, n, 128), bf),
            pltpu.VMEM((4, n + 1024, 128), bf),
            pltpu.VMEM((4, n + 1024, 128), bf),
            pltpu.VMEM((12, n, 128), f32),
            dma((90,)), dma((4, 3)), dma((4, 16)), dma((16,)), dma((2,)), dma((21,)),
            dma((48,)), dma((64,)), dma((64,)), dma((48,)),
            dma((64,)), dma((64,)), dma,
        ],
        compiler_params=pltpu.CompilerParams(
            collective_id=0, has_side_effects=True, vmem_limit_bytes=60 << 20
        ),
        name="layer",
    )(w_qkv, w_out, rows, boxes, count, valid, link, gate)


def per_device(frames_x, box_embed, box_count, frame_valid, cycle_link, w_qkv, w_out, box_gate):
    result = layer(
        w_qkv,
        w_out,
        frames_x.reshape(TOKENS, D),
        box_embed.reshape(16, D),
        box_count,
        frame_valid,
        cycle_link,
        box_gate,
    )
    return result.reshape(frames_x.shape)


def solution(mesh):
    in_specs = (
        P("view", "tm", None, None),
        P("view", "tm", None, None),
        P("view", "tm"),
        P("view", "tm"),
        P("view", None),
        P("tm", None),
        P("tm", None),
        P(),
    )
    out_specs = P("view", "tm", None, None)
    return jax.shard_map(
        per_device, mesh=mesh, in_specs=in_specs, out_specs=out_specs, check_vma=False
    )
```

```python
import jax
import jax.numpy as jnp
from jax import lax
from jax.experimental import pallas as pl
from jax.experimental.pallas import tpu as pltpu
from jax.sharding import PartitionSpec as P

MESH = pl.DeviceIdType.MESH
XC = 768
ZQ = 384
ZW = 1536
QX = 4 * XC
D = 1152
TOKENS = 384
HD = 72
CROSS_HEADS = 8
TIME_HEADS = 4
BOX_HEADS = 4
NEG = -1e30
EXP_SCALE = HD**-0.5 * 1.4426950408889634


def layer_kernel(
    wq, wo, x_ref, box_ref, cnt_ref, val_ref, link_ref, gate_ref, out_ref,
    wx, wz, xn, m, stage,
    qkv, nbr, tsend, tqkv, tout, timed, kvb, bkv, qc, kc, vc, qb, kb, vb, oh,
    ssem, msem, rxs, rzs, nsem, lsem,
    ts_send, ts_recv, to_send, to_recv, br_send, br_recv, own_sem,
):
    bf, f32 = jnp.bfloat16, jnp.float32
    n = TOKENS
    v = lax.axis_index("view")
    t = lax.axis_index("tm")
    core = lax.rem(v, 2)
    x = lax.rem(t, 4)
    z = lax.rem(t // 4, 8)
    yh = t // 32
    d = 1 - 2 * core
    up, down = lax.rem(v + 1, 8), lax.rem(v + 7, 8)
    partner = v + 1 - 2 * core
    v4 = lax.rem(v + 4, 8)
    owner = (t // 4) * 3 + x
    right, left, across = [lax.rem(x + j, 4) for j in (1, 3, 2)]

    def tm(yy, zz, xx):
        return (yy * 8 + zz) * 4 + xx

    def zat(k):
        return lax.rem(z + d * k + 16, 8)

    plane = [tm(yh, z, lax.rem(x + j, 4)) for j in range(1, 4)] + [tm(1 - yh, z, x)]
    barrier = pltpu.get_barrier_semaphore()

    @pl.loop(0, 64)
    def _(i):
        pl.semaphore_signal(barrier, inc=1, device_id=(v4, i), device_id_type=MESH)

    for p in plane + [tm(yh, zat(1), x), tm(yh, zat(-1), x)]:
        pl.semaphore_signal(barrier, inc=1, device_id=(v, p), device_id_type=MESH)
    for p in (up, down):
        pl.semaphore_signal(barrier, inc=1, device_id=(p, t), device_id_type=MESH)
    pl.semaphore_wait(barrier, 72)

    sends = []

    def send(src, dst, rsem, to):
        c = pltpu.make_async_remote_copy(
            src_ref=src,
            dst_ref=dst,
            send_sem=ssem.at[len(sends)],
            recv_sem=rsem,
            device_id=to,
            device_id_type=MESH,
        )
        c.start()
        sends.append(c)

    def arrived(ref, sem):
        pltpu.make_async_copy(ref, ref, sem).wait()

    @pl.when(core == yh)
    def _():
        out = []
        for j in (2, 1, 3, 0):
            xx = lax.rem(x + j, 4)
            cols = pl.ds(pl.multiple_of(xx * XC, 128), XC)
            for half, view in ((1 - yh, v4), (yh, v)):
                for k, (src, lo, width) in enumerate(
                    (
                        (wq.at[:, cols], 0, XC),
                        (wq.at[:, pl.ds(QX, ZQ)], XC, ZQ),
                        (wo, XC + ZQ, ZW - ZQ),
                    )
                ):
                    dst = m.at[x, :, pl.ds(lo, width)]
                    if view is v and j == 0:
                        pltpu.make_async_copy(src, dst, msem.at[x, k]).start()
                        continue
                    c = pltpu.make_async_remote_copy(
                        src_ref=src,
                        dst_ref=dst,
                        send_sem=lsem.at[len(out)],
                        recv_sem=msem.at[x, k],
                        device_id=(view, tm(half, z, xx)),
                        device_id_type=MESH,
                    )
                    c.start()
                    out.append(c)
        for c in out:
            c.wait_send()

    row = lax.broadcasted_iota(jnp.int32, (72, 18), 0)
    col = lax.broadcasted_iota(jnp.int32, (72, 18), 1)
    for xx in range(4):
        arrived(m.at[xx, :, pl.ds(0, XC)], msem.at[xx, 0])
        arrived(m.at[xx, :, pl.ds(XC, ZQ)], msem.at[xx, 1])
        arrived(m.at[xx, :, pl.ds(XC + ZQ, ZW - ZQ)], msem.at[xx, 2])
    acc = jnp.zeros((72, XC + ZW), f32)
    for xx in range(4):
        pick = (row == col + 18 * xx).astype(bf)
        acc += jnp.dot(pick, m[xx], preferred_element_type=f32)
    stage[...] = acc.astype(bf)

    mine = core * 8
    b0 = mine + z
    fresh = [
        pltpu.make_async_copy(stage.at[:, pl.ds(0, XC)], wx.at[x, b0], rxs.at[x, b0]),
        pltpu.make_async_copy(stage.at[:, pl.ds(XC, ZW)], wz.at[b0], rzs.at[b0]),
    ]
    for c in fresh:
        c.start()

    def forward(xx, b, to):
        send(wx.at[xx, b], wx.at[xx, b], rxs.at[xx, b], to)

    def spread_x(b, src, nxt):
        for k in nxt:
            send(src, wx.at[x, b], rxs.at[x, b], (v, tm(yh, k, x)))
        for xx in (right, left):
            send(src, wx.at[x, b], rxs.at[x, b], (v, tm(yh, z, xx)))
        send(src, wx.at[x, b], rxs.at[x, b], (partner, t))

    def spread_z(b, src, nxt):
        for k in nxt:
            send(src, wz.at[b], rzs.at[b], (v, tm(yh, k, x)))
        send(src, wz.at[b], rzs.at[b], (partner, t))

    def relay_x(b, sign):
        arrived(wx.at[left, b], rxs.at[left, b])
        if sign > 0:
            forward(left, b, (v, tm(yh, z, right)))
        forward(left, b, (partner, t))
        arrived(wx.at[right, b], rxs.at[right, b])
        if sign < 0:
            forward(right, b, (v, tm(yh, z, left)))
        forward(right, b, (partner, t))

    def last_x(b):
        arrived(wx.at[across, b], rxs.at[across, b])
        forward(across, b, (partner, t))

    spread_x(b0, stage.at[:, pl.ds(0, XC)], (zat(1), zat(-1)))
    spread_z(b0, stage.at[:, pl.ds(XC, ZW)], (zat(1), zat(-1)))
    send(x_ref, xn.at[0], nsem.at[0], (up, t))
    send(x_ref, xn.at[1], nsem.at[1], (down, t))
    todo, late = [(b0, -1)], []
    for s in range(1, 5):
        signs = (1, -1) if s < 4 else (1,)
        for sign in signs:
            b = mine + zat(-s * sign)
            arrived(wx.at[x, b], rxs.at[x, b])
            spread_x(b, wx.at[x, b], (zat(sign),) if s < (4 if sign > 0 else 3) else ())
        for sign in signs:
            b = mine + zat(-s * sign)
            arrived(wz.at[b], rzs.at[b])
            spread_z(b, wz.at[b], (zat(sign),) if s < (4 if sign > 0 else 3) else ())
            todo.append((b, sign))
            b, sign = todo.pop(0)
            relay_x(b, sign)
            late.append(b)
            if len(late) > 2:
                last_x(late.pop(0))
    for b, sign in todo:
        relay_x(b, sign)
        late.append(b)
    for b in late:
        last_x(b)
    for c in fresh:
        c.wait()
    other = 8 - mine
    for k in range(8):
        b = other + k
        arrived(wz.at[b], rzs.at[b])
        for xx in range(4):
            arrived(wx.at[xx, b], rxs.at[xx, b])

    def mm(a, b):
        return jnp.dot(a, b, preferred_element_type=f32)

    def chunk(i, lo, hi):
        return wx[i, :, :, lo:hi].reshape(D, hi - lo)

    def tail(lo, hi):
        return wz[:, :, lo:hi].reshape(D, hi - lo)

    boxes = box_ref[...]
    bk = jnp.concatenate([mm(boxes, chunk(2, 384, 768)), mm(boxes, tail(0, 384))], axis=1)
    slot = lax.broadcasted_iota(jnp.int32, (16, 768), 0)
    blane = lax.broadcasted_iota(jnp.int32, (16, 768), 1)
    live = jnp.logical_and(slot < cnt_ref[0, 0], val_ref[0, 0] == 1)
    bv = jnp.where(blane < 288, pltpu.roll(bk, 768 - 96, 1), pltpu.roll(bk, 768 - 192, 1))
    bv = jnp.where(blane == 576, jnp.where(live, 0.0, NEG), bv)
    kvb[...] = bv[:, :640].astype(bf)

    rows = x_ref[...]
    spots = (
        (512, chunk(0, 512, 768)),
        (768, chunk(1, 0, 128)),
        (1664, chunk(2, 128, 512)),
        (2816, chunk(3, 512, 768)),
        (3072, tail(0, 128)),
    )
    for lo, w in spots:
        qkv[:, lo : lo + w.shape[1]] = mm(rows, w)
    lane = lax.broadcasted_iota(jnp.int32, (n, 896), 1)
    blank = jnp.zeros((n, 512), f32)
    parts = [
        pltpu.roll(jnp.concatenate([qkv[:, lo : lo + 384], blank], axis=1), shift, 1)
        for lo, shift in ((512, 896 - 64), (1664, 288 - 64), (2816, 576 - 64))
    ]
    packed = jnp.where(lane < 288, parts[0], jnp.where(lane < 576, parts[1], parts[2]))
    tsend[...] = packed.astype(bf).reshape(48, 8, 896)

    def zfar(j):
        k = 7 - j
        h = (k + 1) // 2
        return lax.rem(z + h * (2 * lax.rem(k, 2) - 1) + 8, 8)

    def time_copy(i):
        half, zz, xx = lax.rem(yh + i, 2), zfar(i // 6), lax.rem(x + i // 2, 3)
        o = (half * 8 + zz) * 3 + xx
        return pltpu.make_async_remote_copy(
            src_ref=tsend.at[o],
            dst_ref=tqkv.at[t],
            send_sem=ts_send.at[i],
            recv_sem=ts_recv.at[t],
            device_id=(v4, tm(half, zz, xx)),
            device_id_type=MESH,
        )

    def send_time(lo, hi):
        @pl.loop(lo, hi)
        def _(i):
            time_copy(i).start()

    sent = []

    def pass_on(slot, to, src=None):
        c = pltpu.make_async_remote_copy(
            src_ref=bkv.at[slot] if src is None else src,
            dst_ref=bkv.at[slot],
            send_sem=br_send.at[len(sent)],
            recv_sem=br_recv.at[slot],
            device_id=(v, to),
            device_id_type=MESH,
        )
        c.start()
        sent.append(c)

    def landed(slot):
        arrived(bkv.at[slot], br_recv.at[slot])

    own = pltpu.make_async_copy(kvb, bkv.at[t], own_sem)
    own.start()
    pass_on(t, tm(1 - yh, z, x), kvb)
    for to in (tm(yh, zat(1), x), tm(yh, zat(-1), x), tm(yh, z, right), tm(yh, z, left)):
        pass_on(t, to, kvb)
    send_time(0, 16)

    spots = (
        (0, chunk(0, 0, 512)),
        (896, chunk(1, 128, 768)),
        (1536, chunk(2, 0, 128)),
        (2048, chunk(2, 512, 768)),
        (2304, chunk(3, 0, 512)),
        (3200, tail(128, 384)),
    )
    for lo, w in spots:
        qkv[:, lo : lo + w.shape[1]] = mm(rows, w)

    own.wait()
    landed(tm(1 - yh, z, x))
    for to in (tm(yh, zat(1), x), tm(yh, zat(-1), x), tm(yh, z, right), tm(yh, z, left)):
        pass_on(tm(1 - yh, z, x), to)

    boxes_x, boxes_late = [(z, -1)], []

    def relay(s):
        for sign in (1, -1) if s < 4 else (1,):
            zz = zat(-s * sign)
            for half in (yh, 1 - yh):
                slot = tm(half, zz, x)
                landed(slot)
                if s < (4 if sign > 0 else 3):
                    pass_on(slot, tm(yh, zat(sign), x))
                pass_on(slot, tm(yh, z, right))
                pass_on(slot, tm(yh, z, left))
            boxes_x.append((zz, sign))

    def relay_boxes(keep):
        while len(boxes_x) > keep:
            zz, sign = boxes_x.pop(0)
            for half in (yh, 1 - yh):
                landed(tm(half, zz, left))
                if sign > 0:
                    pass_on(tm(half, zz, left), tm(yh, z, right))
                landed(tm(half, zz, right))
                if sign < 0:
                    pass_on(tm(half, zz, right), tm(yh, z, left))
            boxes_late.append(zz)

    send_time(16, 32)

    arrived(xn.at[0], nsem.at[0])
    arrived(xn.at[1], nsem.at[1])
    near = xn[...].reshape(2 * n, D)
    nbr[:, 0:384] = mm(near, chunk(1, 384, 768))
    nbr[:, 384:640] = mm(near, chunk(2, 0, 256))
    nbr[:, 640:1280] = mm(near, chunk(3, 0, 640))

    relay(1)
    relay_boxes(2)
    send_time(32, 48)

    def tile(a, off, fill):
        piece = pltpu.roll(a, (a.shape[1] - off) % a.shape[1], 1)[:, :128] if off else a[:, :128]
        at = lax.broadcasted_iota(jnp.int32, piece.shape, 1)
        return jnp.where(at < HD, piece, jnp.where(at == HD, fill, 0.0)).astype(bf)

    def head(ref, r0, r1, c, fill):
        lo = c // 128 * 128
        a = ref[r0:r1, lo : min(lo + 256, ref.shape[1])]
        return tile(a, c - lo, fill)

    gone = [jnp.where(link_ref[0, i] > 0, 0.0, NEG) for i in range(2)]
    for h in range(CROSS_HEADS):
        qc[h] = head(qkv, 0, n, HD * h, 1.0)
        for s, (ref, r0, ck, cv, fill) in enumerate(
            (
                (nbr, 0, 0, 640, gone[0]),
                (qkv, 0, D, 2 * D, 0.0),
                (nbr, n, 0, 640, gone[1]),
            )
        ):
            kc[h, s * n : (s + 1) * n] = head(ref, r0, r0 + n, ck + HD * h, fill)
            vc[h, s * n : (s + 1) * n] = head(ref, r0, r0 + n, cv + HD * h, 1.0)
    at0 = (CROSS_HEADS + TIME_HEADS) * HD
    for h in range(BOX_HEADS):
        qb[h] = head(qkv, 0, n, at0 + HD * h, 1.0)
        kb[h, 0:n] = head(qkv, 0, n, D + at0 + HD * h, 0.0)
        vb[h, 0:n] = head(qkv, 0, n, 2 * D + at0 + HD * h, 1.0)

    def softmax_dot(q, k, val):
        s = lax.dot_general(q, k, (((1,), (1,)), ((), ())), preferred_element_type=f32)
        top = jnp.max(s, axis=1, keepdims=True)
        p = jnp.exp2((s - top) * EXP_SCALE).astype(bf)
        return mm(p, val)

    def heads(first_head, count, q_ref, k_ref, v_ref, out0):
        @pl.loop(first_head, first_head + count)
        def _(h):
            for r in range(0, n, 128):
                o = softmax_dot(q_ref[h, r : r + 128], k_ref[h], v_ref[h])
                oh[out0 + h, r : r + 128] = o * (1.0 / o[:, HD : HD + 1])

    for s in range(1, 5):
        if s > 1:
            relay(s)
            relay_boxes(2)
        heads(2 * (s - 1), 2, qc, kc, vc, 0)
    relay_boxes(0)

    @pl.loop(0, 64)
    def _(i):
        ref = tqkv.at[i]

        @pl.when(x < 3)
        def _():
            pltpu.make_async_copy(ref, ref, ts_recv.at[i]).wait()

    def back(i):
        f = tm(lax.rem(yh + i, 2), zfar(i // 8), lax.rem(x + i // 2, 4))
        return pltpu.make_async_remote_copy(
            src_ref=tout.at[f],
            dst_ref=timed.at[owner],
            send_sem=to_send.at[i],
            recv_sem=to_recv.at[owner],
            device_id=(v4, f),
            device_id_type=MESH,
        )

    @pl.when(x < 3)
    def _():
        a = tqkv[...].reshape(512, 896).astype(f32)
        r = lax.broadcasted_iota(jnp.int32, (512, 512), 0)
        c = lax.broadcasted_iota(jnp.int32, (512, 512), 1)
        other = jnp.where(jnp.bitwise_and(r, 7) == jnp.bitwise_and(c, 7), 0.0, NEG)
        outs = []
        for h in range(TIME_HEADS):
            q = tile(a, HD * h, 0.0)
            k = tile(a, 288 + HD * h, 0.0)
            val = tile(a, 576 + HD * h, 1.0)
            s = lax.dot_general(q, k, (((1,), (1,)), ((), ())), preferred_element_type=f32) + other
            top = jnp.max(s, axis=1, keepdims=True)
            p = jnp.exp2((s - top) * EXP_SCALE).astype(bf)
            o = mm(p, val)
            outs.append(o * (1.0 / o[:, HD : HD + 1]))
        tout[...] = joined(outs).astype(bf).reshape(64, 8, 384)

    for zz in boxes_late:
        for half in (yh, 1 - yh):
            landed(tm(half, zz, across))
    for r in range(0, 1024, 256):
        a = bkv[r // 16 : r // 16 + 16].reshape(256, 640).astype(f32)
        fill = a[:, 576:577]
        for h in range(BOX_HEADS):
            kb[h, n + r : n + r + 256] = tile(a, HD * h, fill)
            vb[h, n + r : n + r + 256] = tile(a, 288 + HD * h, 1.0)

    @pl.when(x < 3)
    def _():
        @pl.loop(0, 64)
        def _(i):
            back(i).start()

    heads(0, BOX_HEADS, qb, kb, vb, CROSS_HEADS)

    total = rows.astype(f32)
    crossed = joined([oh[h] for h in range(CROSS_HEADS)]).astype(bf)
    total += mm(crossed[:, :576], wz[0:8, :, ZQ:ZW].reshape(576, D))
    boxed = joined([oh[CROSS_HEADS + h] for h in range(BOX_HEADS)])[:, :288]
    boxed = (boxed * jnp.tanh(gate_ref[...].reshape(1, BOX_HEADS * HD))).astype(bf)
    total += mm(boxed, wz[12:16, :, ZQ:ZW].reshape(288, D))

    @pl.loop(0, 48)
    def _(i):
        ref = timed.at[i]
        pltpu.make_async_copy(ref, ref, to_recv.at[i]).wait()

    both = timed[...].reshape(n, 384)
    total += mm(both[:, :288], wz[8:12, :, ZQ:ZW].reshape(288, D))
    out_ref[...] = total.astype(bf)

    @pl.loop(0, 48)
    def _(i):
        time_copy(i).wait_send()

    @pl.when(x < 3)
    def _():
        @pl.loop(0, 64)
        def _(i):
            back(i).wait_send()

    for c in sends + sent:
        c.wait_send()


def joined(outs):
    width = -(-len(outs) * HD // 128) * 128
    rows = outs[0].shape[0]
    at = lax.broadcasted_iota(jnp.int32, (rows, 128), 1)
    blank = jnp.zeros((rows, 128), jnp.float32)
    done = []
    for c in range(width // 128):
        piece = blank
        for h, o in enumerate(outs):
            lo = h * HD - c * 128
            if lo >= 128 or lo + HD <= 0:
                continue
            moved = pltpu.roll(o, lo % 128, 1) if lo % 128 else o
            keep = jnp.logical_and(at >= lo, at < lo + HD)
            piece = jnp.where(keep, moved, piece)
        done.append(piece)
    return jnp.concatenate(done, axis=1)


def layer(w_qkv, w_out, rows, boxes, count, valid, link, gate):
    bf, f32 = jnp.bfloat16, jnp.float32
    hbm = pl.BlockSpec(memory_space=pl.ANY)
    vmem = pl.BlockSpec(memory_space=pltpu.VMEM)
    smem = pl.BlockSpec(memory_space=pltpu.SMEM)
    n = TOKENS
    dma = pltpu.SemaphoreType.DMA
    return pl.pallas_call(
        layer_kernel,
        out_shape=jax.ShapeDtypeStruct(rows.shape, bf),
        in_specs=[hbm] * 2 + [vmem] * 2 + [smem] * 3 + [vmem],
        out_specs=vmem,
        scratch_shapes=[
            pltpu.VMEM((4, 16, 72, XC), bf),
            pltpu.VMEM((16, 72, ZW), bf),
            pltpu.VMEM((2, n, D), bf),
            pltpu.VMEM((4, 18, XC + ZW), bf),
            pltpu.VMEM((72, XC + ZW), bf),
            pltpu.VMEM((n, 3 * D), f32),
            pltpu.VMEM((2 * n, 1280), f32),
            pltpu.VMEM((48, 8, 896), bf),
            pltpu.VMEM((64, 8, 896), bf),
            pltpu.VMEM((64, 8, 384), bf),
            pltpu.VMEM((48, 8, 384), bf),
            pltpu.VMEM((16, 640), bf),
            pltpu.VMEM((64, 16, 640), bf),
            pltpu.VMEM((8, n, 128), bf),
            pltpu.VMEM((8, 3 * n, 128), bf),
            pltpu.VMEM((8, 3 * n, 128), bf),
            pltpu.VMEM((4, n, 128), bf),
            pltpu.VMEM((4, n + 1024, 128), bf),
            pltpu.VMEM((4, n + 1024, 128), bf),
            pltpu.VMEM((12, n, 128), f32),
            dma((90,)), dma((4, 3)), dma((4, 16)), dma((16,)), dma((2,)), dma((21,)),
            dma((48,)), dma((64,)), dma((64,)), dma((48,)),
            dma((64,)), dma((64,)), dma,
        ],
        compiler_params=pltpu.CompilerParams(
            collective_id=0, has_side_effects=True, vmem_limit_bytes=60 << 20
        ),
        name="layer",
    )(w_qkv, w_out, rows, boxes, count, valid, link, gate)


def per_device(frames_x, box_embed, box_count, frame_valid, cycle_link, w_qkv, w_out, box_gate):
    result = layer(
        w_qkv,
        w_out,
        frames_x.reshape(TOKENS, D),
        box_embed.reshape(16, D),
        box_count,
        frame_valid,
        cycle_link,
        box_gate,
    )
    return result.reshape(frames_x.shape)


def solution(mesh):
    in_specs = (
        P("view", "tm", None, None),
        P("view", "tm", None, None),
        P("view", "tm"),
        P("view", "tm"),
        P("view", None),
        P("tm", None),
        P("tm", None),
        P(),
    )
    out_specs = P("view", "tm", None, None)
    return jax.shard_map(
        per_device, mesh=mesh, in_specs=in_specs, out_specs=out_specs, check_vma=False
    )
```

```python
import jax
import jax.numpy as jnp
from jax import lax
from jax.experimental import pallas as pl
from jax.experimental.pallas import tpu as pltpu
from jax.sharding import PartitionSpec as P

MESH = pl.DeviceIdType.MESH
XC = 768
ZQ = 384
ZW = 1536
QX = 4 * XC
D = 1152
TOKENS = 384
HD = 72
CROSS_HEADS = 8
TIME_HEADS = 4
BOX_HEADS = 4
NEG = -1e30
EXP_SCALE = HD**-0.5 * 1.4426950408889634


def layer_kernel(
    wq, wo, x_ref, box_ref, cnt_ref, val_ref, link_ref, gate_ref, out_ref,
    wx, wz, xn, m, stage,
    qkv, nbr, tsend, tqkv, tout, timed, kvb, bkv, qc, kc, vc, qb, kb, vb, oh,
    ssem, msem, rxs, rzs, nsem, lsem,
    ts_send, ts_recv, to_send, to_recv, br_send, br_recv, own_sem,
):
    bf, f32 = jnp.bfloat16, jnp.float32
    n = TOKENS
    v = lax.axis_index("view")
    t = lax.axis_index("tm")
    core = lax.rem(v, 2)
    x = lax.rem(t, 4)
    z = lax.rem(t // 4, 8)
    yh = t // 32
    d = 1 - 2 * core
    up, down = lax.rem(v + 1, 8), lax.rem(v + 7, 8)
    partner = v + 1 - 2 * core
    v4 = lax.rem(v + 4, 8)
    owner = (t // 4) * 3 + x
    right, left, across = [lax.rem(x + j, 4) for j in (1, 3, 2)]

    def tm(yy, zz, xx):
        return (yy * 8 + zz) * 4 + xx

    def zat(k):
        return lax.rem(z + d * k + 16, 8)

    plane = [tm(yh, z, lax.rem(x + j, 4)) for j in range(1, 4)] + [tm(1 - yh, z, x)]
    barrier = pltpu.get_barrier_semaphore()

    @pl.loop(0, 64)
    def _(i):
        pl.semaphore_signal(barrier, inc=1, device_id=(v4, i), device_id_type=MESH)

    for p in plane + [tm(yh, zat(1), x), tm(yh, zat(-1), x)]:
        pl.semaphore_signal(barrier, inc=1, device_id=(v, p), device_id_type=MESH)
    for p in (up, down):
        pl.semaphore_signal(barrier, inc=1, device_id=(p, t), device_id_type=MESH)
    pl.semaphore_wait(barrier, 72)

    sends = []

    def send(src, dst, rsem, to):
        c = pltpu.make_async_remote_copy(
            src_ref=src,
            dst_ref=dst,
            send_sem=ssem.at[len(sends)],
            recv_sem=rsem,
            device_id=to,
            device_id_type=MESH,
        )
        c.start()
        sends.append(c)

    def arrived(ref, sem):
        pltpu.make_async_copy(ref, ref, sem).wait()

    @pl.when(core == yh)
    def _():
        out = []
        for j in (2, 1, 3, 0):
            xx = lax.rem(x + j, 4)
            cols = pl.ds(pl.multiple_of(xx * XC, 128), XC)
            for half, view in ((1 - yh, v4), (yh, v)):
                for k, (src, lo, width) in enumerate(
                    (
                        (wq.at[:, cols], 0, XC),
                        (wq.at[:, pl.ds(QX, ZQ)], XC, ZQ),
                        (wo, XC + ZQ, ZW - ZQ),
                    )
                ):
                    dst = m.at[x, :, pl.ds(lo, width)]
                    if view is v and j == 0:
                        pltpu.make_async_copy(src, dst, msem.at[x, k]).start()
                        continue
                    c = pltpu.make_async_remote_copy(
                        src_ref=src,
                        dst_ref=dst,
                        send_sem=lsem.at[len(out)],
                        recv_sem=msem.at[x, k],
                        device_id=(view, tm(half, z, xx)),
                        device_id_type=MESH,
                    )
                    c.start()
                    out.append(c)
        for c in out:
            c.wait_send()

    row = lax.broadcasted_iota(jnp.int32, (72, 18), 0)
    col = lax.broadcasted_iota(jnp.int32, (72, 18), 1)
    for xx in range(4):
        arrived(m.at[xx, :, pl.ds(0, XC)], msem.at[xx, 0])
        arrived(m.at[xx, :, pl.ds(XC, ZQ)], msem.at[xx, 1])
        arrived(m.at[xx, :, pl.ds(XC + ZQ, ZW - ZQ)], msem.at[xx, 2])
    acc = jnp.zeros((72, XC + ZW), f32)
    for xx in range(4):
        pick = (row == col + 18 * xx).astype(bf)
        acc += jnp.dot(pick, m[xx], preferred_element_type=f32)
    stage[...] = acc.astype(bf)

    mine = core * 8
    b0 = mine + z
    fresh = [
        pltpu.make_async_copy(stage.at[:, pl.ds(0, XC)], wx.at[x, b0], rxs.at[x, b0]),
        pltpu.make_async_copy(stage.at[:, pl.ds(XC, ZW)], wz.at[b0], rzs.at[b0]),
    ]
    for c in fresh:
        c.start()

    def forward(xx, b, to):
        send(wx.at[xx, b], wx.at[xx, b], rxs.at[xx, b], to)

    def spread_x(b, src, nxt):
        for k in nxt:
            send(src, wx.at[x, b], rxs.at[x, b], (v, tm(yh, k, x)))
        for xx in (right, left):
            send(src, wx.at[x, b], rxs.at[x, b], (v, tm(yh, z, xx)))
        send(src, wx.at[x, b], rxs.at[x, b], (partner, t))

    def spread_z(b, src, nxt):
        for k in nxt:
            send(src, wz.at[b], rzs.at[b], (v, tm(yh, k, x)))
        send(src, wz.at[b], rzs.at[b], (partner, t))

    def relay_x(b, sign):
        arrived(wx.at[left, b], rxs.at[left, b])
        if sign > 0:
            forward(left, b, (v, tm(yh, z, right)))
        forward(left, b, (partner, t))
        arrived(wx.at[right, b], rxs.at[right, b])
        if sign < 0:
            forward(right, b, (v, tm(yh, z, left)))
        forward(right, b, (partner, t))

    def last_x(b):
        arrived(wx.at[across, b], rxs.at[across, b])
        forward(across, b, (partner, t))

    spread_x(b0, stage.at[:, pl.ds(0, XC)], (zat(1), zat(-1)))
    spread_z(b0, stage.at[:, pl.ds(XC, ZW)], (zat(1), zat(-1)))
    send(x_ref, xn.at[0], nsem.at[0], (up, t))
    send(x_ref, xn.at[1], nsem.at[1], (down, t))
    todo, late = [(b0, -1)], []
    for s in range(1, 5):
        signs = (1, -1) if s < 4 else (1,)
        for sign in signs:
            b = mine + zat(-s * sign)
            arrived(wx.at[x, b], rxs.at[x, b])
            spread_x(b, wx.at[x, b], (zat(sign),) if s < (4 if sign > 0 else 3) else ())
        for sign in signs:
            b = mine + zat(-s * sign)
            arrived(wz.at[b], rzs.at[b])
            spread_z(b, wz.at[b], (zat(sign),) if s < (4 if sign > 0 else 3) else ())
            todo.append((b, sign))
            b, sign = todo.pop(0)
            relay_x(b, sign)
            late.append(b)
            if len(late) > 2:
                last_x(late.pop(0))
    for b, sign in todo:
        relay_x(b, sign)
        late.append(b)
    for b in late:
        last_x(b)
    for c in fresh:
        c.wait()
    other = 8 - mine
    for k in range(8):
        b = other + k
        arrived(wz.at[b], rzs.at[b])
        for xx in range(4):
            arrived(wx.at[xx, b], rxs.at[xx, b])

    def mm(a, b):
        return jnp.dot(a, b, preferred_element_type=f32)

    def chunk(i, lo, hi):
        return wx[i, :, :, lo:hi].reshape(D, hi - lo)

    def tail(lo, hi):
        return wz[:, :, lo:hi].reshape(D, hi - lo)

    boxes = box_ref[...]
    bk = jnp.concatenate([mm(boxes, chunk(2, 384, 768)), mm(boxes, tail(0, 384))], axis=1)
    slot = lax.broadcasted_iota(jnp.int32, (16, 768), 0)
    blane = lax.broadcasted_iota(jnp.int32, (16, 768), 1)
    live = jnp.logical_and(slot < cnt_ref[0, 0], val_ref[0, 0] == 1)
    bv = jnp.where(blane < 288, pltpu.roll(bk, 768 - 96, 1), pltpu.roll(bk, 768 - 192, 1))
    bv = jnp.where(blane == 576, jnp.where(live, 0.0, NEG), bv)
    kvb[...] = bv[:, :640].astype(bf)

    rows = x_ref[...]
    spots = (
        (512, chunk(0, 512, 768)),
        (768, chunk(1, 0, 128)),
        (1664, chunk(2, 128, 512)),
        (2816, chunk(3, 512, 768)),
        (3072, tail(0, 128)),
    )
    for lo, w in spots:
        qkv[:, lo : lo + w.shape[1]] = mm(rows, w)
    lane = lax.broadcasted_iota(jnp.int32, (n, 896), 1)
    blank = jnp.zeros((n, 512), f32)
    parts = [
        pltpu.roll(jnp.concatenate([qkv[:, lo : lo + 384], blank], axis=1), shift, 1)
        for lo, shift in ((512, 896 - 64), (1664, 288 - 64), (2816, 576 - 64))
    ]
    packed = jnp.where(lane < 288, parts[0], jnp.where(lane < 576, parts[1], parts[2]))
    tsend[...] = packed.astype(bf).reshape(48, 8, 896)

    def zfar(j):
        k = 7 - j
        h = (k + 1) // 2
        return lax.rem(z + h * (2 * lax.rem(k, 2) - 1) + 8, 8)

    def time_copy(i):
        half, zz, xx = lax.rem(yh + i, 2), zfar(i // 6), lax.rem(x + i // 2, 3)
        o = (half * 8 + zz) * 3 + xx
        return pltpu.make_async_remote_copy(
            src_ref=tsend.at[o],
            dst_ref=tqkv.at[t],
            send_sem=ts_send.at[i],
            recv_sem=ts_recv.at[t],
            device_id=(v4, tm(half, zz, xx)),
            device_id_type=MESH,
        )

    def send_time(lo, hi):
        @pl.loop(lo, hi)
        def _(i):
            time_copy(i).start()

    sent = []

    def pass_on(slot, to, src=None):
        c = pltpu.make_async_remote_copy(
            src_ref=bkv.at[slot] if src is None else src,
            dst_ref=bkv.at[slot],
            send_sem=br_send.at[len(sent)],
            recv_sem=br_recv.at[slot],
            device_id=(v, to),
            device_id_type=MESH,
        )
        c.start()
        sent.append(c)

    def landed(slot):
        arrived(bkv.at[slot], br_recv.at[slot])

    own = pltpu.make_async_copy(kvb, bkv.at[t], own_sem)
    own.start()
    pass_on(t, tm(1 - yh, z, x), kvb)
    for to in (tm(yh, zat(1), x), tm(yh, zat(-1), x), tm(yh, z, right), tm(yh, z, left)):
        pass_on(t, to, kvb)
    send_time(0, 16)

    spots = (
        (0, chunk(0, 0, 512)),
        (896, chunk(1, 128, 768)),
        (1536, chunk(2, 0, 128)),
        (2048, chunk(2, 512, 768)),
        (2304, chunk(3, 0, 512)),
        (3200, tail(128, 384)),
    )
    for lo, w in spots:
        qkv[:, lo : lo + w.shape[1]] = mm(rows, w)

    own.wait()
    landed(tm(1 - yh, z, x))
    for to in (tm(yh, zat(1), x), tm(yh, zat(-1), x), tm(yh, z, right), tm(yh, z, left)):
        pass_on(tm(1 - yh, z, x), to)

    boxes_x, boxes_late = [(z, -1)], []

    def relay(s):
        for sign in (1, -1) if s < 4 else (1,):
            zz = zat(-s * sign)
            for half in (yh, 1 - yh):
                slot = tm(half, zz, x)
                landed(slot)
                if s < (4 if sign > 0 else 3):
                    pass_on(slot, tm(yh, zat(sign), x))
                pass_on(slot, tm(yh, z, right))
                pass_on(slot, tm(yh, z, left))
            boxes_x.append((zz, sign))

    def relay_boxes(keep):
        while len(boxes_x) > keep:
            zz, sign = boxes_x.pop(0)
            for half in (yh, 1 - yh):
                landed(tm(half, zz, left))
                if sign > 0:
                    pass_on(tm(half, zz, left), tm(yh, z, right))
                landed(tm(half, zz, right))
                if sign < 0:
                    pass_on(tm(half, zz, right), tm(yh, z, left))
            boxes_late.append(zz)

    send_time(16, 32)

    arrived(xn.at[0], nsem.at[0])
    arrived(xn.at[1], nsem.at[1])
    near = xn[...].reshape(2 * n, D)
    nbr[:, 0:384] = mm(near, chunk(1, 384, 768))
    nbr[:, 384:640] = mm(near, chunk(2, 0, 256))
    nbr[:, 640:1280] = mm(near, chunk(3, 0, 640))

    relay(1)
    relay_boxes(2)
    send_time(32, 48)

    def tile(a, off, fill):
        piece = pltpu.roll(a, (a.shape[1] - off) % a.shape[1], 1)[:, :128] if off else a[:, :128]
        at = lax.broadcasted_iota(jnp.int32, piece.shape, 1)
        return jnp.where(at < HD, piece, jnp.where(at == HD, fill, 0.0)).astype(bf)

    def head(ref, r0, r1, c, fill):
        lo = c // 128 * 128
        a = ref[r0:r1, lo : min(lo + 256, ref.shape[1])]
        return tile(a, c - lo, fill)

    gone = [jnp.where(link_ref[0, i] > 0, 0.0, NEG) for i in range(2)]
    for h in range(CROSS_HEADS):
        qc[h] = head(qkv, 0, n, HD * h, 1.0)
        for s, (ref, r0, ck, cv, fill) in enumerate(
            (
                (nbr, 0, 0, 640, gone[0]),
                (qkv, 0, D, 2 * D, 0.0),
                (nbr, n, 0, 640, gone[1]),
            )
        ):
            kc[h, s * n : (s + 1) * n] = head(ref, r0, r0 + n, ck + HD * h, fill)
            vc[h, s * n : (s + 1) * n] = head(ref, r0, r0 + n, cv + HD * h, 1.0)
    at0 = (CROSS_HEADS + TIME_HEADS) * HD
    for h in range(BOX_HEADS):
        qb[h] = head(qkv, 0, n, at0 + HD * h, 1.0)
        kb[h, 0:n] = head(qkv, 0, n, D + at0 + HD * h, 0.0)
        vb[h, 0:n] = head(qkv, 0, n, 2 * D + at0 + HD * h, 1.0)

    def softmax_dot(q, k, val):
        s = lax.dot_general(q, k, (((1,), (1,)), ((), ())), preferred_element_type=f32)
        top = jnp.max(s, axis=1, keepdims=True)
        p = jnp.exp2((s - top) * EXP_SCALE).astype(bf)
        return mm(p, val)

    def heads(first_head, count, q_ref, k_ref, v_ref, out0):
        @pl.loop(first_head, first_head + count)
        def _(h):
            for r in range(0, n, 128):
                o = softmax_dot(q_ref[h, r : r + 128], k_ref[h], v_ref[h])
                oh[out0 + h, r : r + 128] = o * (1.0 / o[:, HD : HD + 1])

    for s in range(1, 5):
        if s > 1:
            relay(s)
            relay_boxes(2)
        heads(2 * (s - 1), 2, qc, kc, vc, 0)
    relay_boxes(0)

    @pl.loop(0, 64)
    def _(i):
        ref = tqkv.at[i]

        @pl.when(x < 3)
        def _():
            pltpu.make_async_copy(ref, ref, ts_recv.at[i]).wait()

    def back(i):
        f = tm(lax.rem(yh + i, 2), zfar(i // 8), lax.rem(x + i // 2, 4))
        return pltpu.make_async_remote_copy(
            src_ref=tout.at[f],
            dst_ref=timed.at[owner],
            send_sem=to_send.at[i],
            recv_sem=to_recv.at[owner],
            device_id=(v4, f),
            device_id_type=MESH,
        )

    @pl.when(x < 3)
    def _():
        a = tqkv[...].reshape(512, 896).astype(f32)
        r = lax.broadcasted_iota(jnp.int32, (512, 512), 0)
        c = lax.broadcasted_iota(jnp.int32, (512, 512), 1)
        other = jnp.where(jnp.bitwise_and(r, 7) == jnp.bitwise_and(c, 7), 0.0, NEG)
        outs = []
        for h in range(TIME_HEADS):
            q = tile(a, HD * h, 0.0)
            k = tile(a, 288 + HD * h, 0.0)
            val = tile(a, 576 + HD * h, 1.0)
            s = lax.dot_general(q, k, (((1,), (1,)), ((), ())), preferred_element_type=f32) + other
            top = jnp.max(s, axis=1, keepdims=True)
            p = jnp.exp2((s - top) * EXP_SCALE).astype(bf)
            o = mm(p, val)
            outs.append(o * (1.0 / o[:, HD : HD + 1]))
        tout[...] = joined(outs).astype(bf).reshape(64, 8, 384)

    @pl.when(x < 3)
    def _():
        @pl.loop(0, 64)
        def _(i):
            back(i).start()

    for zz in boxes_late:
        for half in (yh, 1 - yh):
            landed(tm(half, zz, across))
    for r in range(0, 1024, 256):
        a = bkv[r // 16 : r // 16 + 16].reshape(256, 640).astype(f32)
        fill = a[:, 576:577]
        for h in range(BOX_HEADS):
            kb[h, n + r : n + r + 256] = tile(a, HD * h, fill)
            vb[h, n + r : n + r + 256] = tile(a, 288 + HD * h, 1.0)

    heads(0, BOX_HEADS, qb, kb, vb, CROSS_HEADS)

    total = rows.astype(f32)
    crossed = joined([oh[h] for h in range(CROSS_HEADS)]).astype(bf)
    total += mm(crossed[:, :576], wz[0:8, :, ZQ:ZW].reshape(576, D))
    boxed = joined([oh[CROSS_HEADS + h] for h in range(BOX_HEADS)])[:, :288]
    boxed = (boxed * jnp.tanh(gate_ref[...].reshape(1, BOX_HEADS * HD))).astype(bf)
    total += mm(boxed, wz[12:16, :, ZQ:ZW].reshape(288, D))

    @pl.loop(0, 48)
    def _(i):
        ref = timed.at[i]
        pltpu.make_async_copy(ref, ref, to_recv.at[i]).wait()

    both = timed[...].reshape(n, 384)
    total += mm(both[:, :288], wz[8:12, :, ZQ:ZW].reshape(288, D))
    out_ref[...] = total.astype(bf)

    @pl.loop(0, 48)
    def _(i):
        time_copy(i).wait_send()

    @pl.when(x < 3)
    def _():
        @pl.loop(0, 64)
        def _(i):
            back(i).wait_send()

    for c in sends + sent:
        c.wait_send()


def joined(outs):
    width = -(-len(outs) * HD // 128) * 128
    rows = outs[0].shape[0]
    at = lax.broadcasted_iota(jnp.int32, (rows, 128), 1)
    blank = jnp.zeros((rows, 128), jnp.float32)
    done = []
    for c in range(width // 128):
        piece = blank
        for h, o in enumerate(outs):
            lo = h * HD - c * 128
            if lo >= 128 or lo + HD <= 0:
                continue
            moved = pltpu.roll(o, lo % 128, 1) if lo % 128 else o
            keep = jnp.logical_and(at >= lo, at < lo + HD)
            piece = jnp.where(keep, moved, piece)
        done.append(piece)
    return jnp.concatenate(done, axis=1)


def layer(w_qkv, w_out, rows, boxes, count, valid, link, gate):
    bf, f32 = jnp.bfloat16, jnp.float32
    hbm = pl.BlockSpec(memory_space=pl.ANY)
    vmem = pl.BlockSpec(memory_space=pltpu.VMEM)
    smem = pl.BlockSpec(memory_space=pltpu.SMEM)
    n = TOKENS
    dma = pltpu.SemaphoreType.DMA
    return pl.pallas_call(
        layer_kernel,
        out_shape=jax.ShapeDtypeStruct(rows.shape, bf),
        in_specs=[hbm] * 2 + [vmem] * 2 + [smem] * 3 + [vmem],
        out_specs=vmem,
        scratch_shapes=[
            pltpu.VMEM((4, 16, 72, XC), bf),
            pltpu.VMEM((16, 72, ZW), bf),
            pltpu.VMEM((2, n, D), bf),
            pltpu.VMEM((4, 18, XC + ZW), bf),
            pltpu.VMEM((72, XC + ZW), bf),
            pltpu.VMEM((n, 3 * D), f32),
            pltpu.VMEM((2 * n, 1280), f32),
            pltpu.VMEM((48, 8, 896), bf),
            pltpu.VMEM((64, 8, 896), bf),
            pltpu.VMEM((64, 8, 384), bf),
            pltpu.VMEM((48, 8, 384), bf),
            pltpu.VMEM((16, 640), bf),
            pltpu.VMEM((64, 16, 640), bf),
            pltpu.VMEM((8, n, 128), bf),
            pltpu.VMEM((8, 3 * n, 128), bf),
            pltpu.VMEM((8, 3 * n, 128), bf),
            pltpu.VMEM((4, n, 128), bf),
            pltpu.VMEM((4, n + 1024, 128), bf),
            pltpu.VMEM((4, n + 1024, 128), bf),
            pltpu.VMEM((12, n, 128), f32),
            dma((90,)), dma((4, 3)), dma((4, 16)), dma((16,)), dma((2,)), dma((21,)),
            dma((48,)), dma((64,)), dma((64,)), dma((48,)),
            dma((64,)), dma((64,)), dma,
        ],
        compiler_params=pltpu.CompilerParams(
            collective_id=0, has_side_effects=True, vmem_limit_bytes=60 << 20
        ),
        name="layer",
    )(w_qkv, w_out, rows, boxes, count, valid, link, gate)


def per_device(frames_x, box_embed, box_count, frame_valid, cycle_link, w_qkv, w_out, box_gate):
    result = layer(
        w_qkv,
        w_out,
        frames_x.reshape(TOKENS, D),
        box_embed.reshape(16, D),
        box_count,
        frame_valid,
        cycle_link,
        box_gate,
    )
    return result.reshape(frames_x.shape)


def solution(mesh):
    in_specs = (
        P("view", "tm", None, None),
        P("view", "tm", None, None),
        P("view", "tm"),
        P("view", "tm"),
        P("view", None),
        P("tm", None),
        P("tm", None),
        P(),
    )
    out_specs = P("view", "tm", None, None)
    return jax.shard_map(
        per_device, mesh=mesh, in_specs=in_specs, out_specs=out_specs, check_vma=False
    )
```
